256 devices in a mesh: seq: 64 (over x_lo, y, z), chan: 4 (over x_hi, core).
Axes of the slice: x: 4 (x_hi: 2, x_lo: 2; x = x_hi * 2 + x_lo), y: 4, z: 8, core: 2. Of those that a mesh axis runs over, the one named last changes fastest.
Arguments:
- query_proj: bfloat16 [8192, 4096], P('seq', 'chan'), may hold values from -6 to 6
- key_proj: bfloat16 [8192, 4096], P('seq', 'chan'), may hold values from -6 to 6
- value_proj: bfloat16 [8192, 4096], P('seq', 'chan'), may hold values from -6 to 6
- short_taps: float32 [3, 3, 4096], P(None, None, 'chan'), may hold values from -2.5 to 2.5
- skip_gain: float32 [4096], P('chan'), may hold values from 0.5 to 1.5
- long_filter: float32 [4096, 8192], P(('chan', 'seq')), may hold values from -1024 to 1024
- out_grad: bfloat16 [8192, 4096], P('seq', 'chan'), may hold values from -6 to 6
Outputs:
- mixed_out: bfloat16 [8192, 4096], P('seq', 'chan')
- query_grad: bfloat16 [8192, 4096], P('seq', 'chan')
- key_grad: bfloat16 [8192, 4096], P('seq', 'chan')
- value_grad: bfloat16 [8192, 4096], P('seq', 'chan')
- filter_grad: float32 [4096, 8192], P(('chan', 'seq'))
The draws below stay inside these ranges and needn't reach their ends.
All inputs are finite; a program needn't handle non-finite values.
Results may differ from the reference program's by a relative error of at most 0.0075.
Values may be sent and summed in bfloat16 or wider, within the bound.
No kernel may reach another device: no remote copies, remote signals or barrier semaphores. Data moves between devices by JAX's collectives and lax.ppermute only.
A program may use at most 64 MiB of HBM per device.

```python
import math
import jax
import jax.numpy as jnp

MODEL_WIDTH = 4096
SHORT = 3
SEQUENCE_LENGTH = 8192


def draw_long_filter(key, part):
    random_subkeys = jax.random.split(key, 6)
    lag_axis = jnp.arange(SEQUENCE_LENGTH, dtype=jnp.float32)[None, :]
    slow_share = 0.5
    roughness = jax.random.truncated_normal(random_subkeys[0], -4.0, 4.0, (MODEL_WIDTH, SEQUENCE_LENGTH), jnp.float32)
    slow_mask = jax.random.bernoulli(random_subkeys[1], slow_share, (MODEL_WIDTH, 1))
    slow_rate = jnp.exp(jax.random.uniform(random_subkeys[2], (MODEL_WIDTH, 1), jnp.float32, math.log(0.2 / SEQUENCE_LENGTH), math.log(2.0 / SEQUENCE_LENGTH)))
    fast_rate = jnp.exp(jax.random.uniform(random_subkeys[3], (MODEL_WIDTH, 1), jnp.float32, math.log(1.0 / 50.0), math.log(1.0 / 20.0)))
    decay_rate = jnp.where(slow_mask, slow_rate, fast_rate)
    envelope = jnp.exp(-decay_rate * lag_axis)
    for pulse_index in range(3):
        starting_delay = jax.random.randint(jax.random.fold_in(random_subkeys[4], pulse_index), (MODEL_WIDTH, 1), 1, SEQUENCE_LENGTH).astype(jnp.float32)
        multiplier = jax.random.uniform(jax.random.fold_in(random_subkeys[5], pulse_index), (MODEL_WIDTH, 1), jnp.float32, 0.5, 0.8)
        envelope = envelope * jnp.where(lag_axis >= starting_delay, multiplier, 1.0)
    energy = (1.0 - jnp.exp(-2.0 * decay_rate * SEQUENCE_LENGTH)) / (1.0 - jnp.exp(-2.0 * decay_rate))
    return roughness * envelope * (math.sqrt(SEQUENCE_LENGTH) / jnp.sqrt(energy))


def level_of(rng, extent, shards, low, largest):
    gain = 1.0
    for dim, blocks in shards:
        steps = jax.random.uniform(jax.random.fold_in(jax.random.fold_in(rng, 6), dim), (blocks,), jnp.float32, low / len(shards), largest / len(shards))
        gain = gain * jnp.repeat(jnp.exp(steps), extent[dim] // blocks).reshape((-1,) + (1,) * (len(extent) - 1 - dim))
    return gain


def gaussian(key, dims, spread, reach, shards=(), held_as=jnp.bfloat16):
    values = jax.random.normal(key, dims, jnp.float32) * spread
    if len(shards) > 0:
        values = level_of(key, dims, shards, -0.22, 0.18) * values
    return jnp.clip(values, min=-reach, max=reach).astype(held_as)


def setup_inputs(seed: int = 0) -> dict:
    keys = jax.random.split(jax.random.key(seed), 8)
    query_proj = gaussian(keys[0], (SEQUENCE_LENGTH, MODEL_WIDTH), 1.0, 6.0, ((0, 64), (1, 4)))
    key_proj = gaussian(keys[1], (SEQUENCE_LENGTH, MODEL_WIDTH), 1.0, 6.0, ((0, 64), (1, 4)))
    value_proj = gaussian(keys[2], (SEQUENCE_LENGTH, MODEL_WIDTH), 1.0, 6.0, ((0, 64), (1, 4)))
    short_taps = gaussian(keys[3], (3, SHORT, MODEL_WIDTH), 0.6, 2.5, ((2, 4),), jnp.float32)
    skip_gain = jnp.clip(0.5 + 1.0 * jax.random.uniform(keys[4], (MODEL_WIDTH,), jnp.float32) ** level_of(keys[4], (MODEL_WIDTH,), ((0, 4),), -0.2, 0.2), 0.5, 1.5)
    long_filter = draw_long_filter(jax.random.fold_in(keys[7], 71), 0)
    out_grad = gaussian(keys[6], (SEQUENCE_LENGTH, MODEL_WIDTH), 1.0, 6.0, ((0, 64), (1, 4)))
    return {"query_proj": query_proj, "key_proj": key_proj, "value_proj": value_proj, "short_taps": short_taps, "skip_gain": skip_gain, "long_filter": long_filter, "out_grad": out_grad}


def causal_taps(signal, weights):
    length = signal.shape[0]
    padded = jnp.concatenate([jnp.zeros((2, signal.shape[1]), signal.dtype), signal], 0)
    return weights[0] * padded[2:length + 2] + weights[1] * padded[1:length + 1] + weights[2] * padded[0:length]

def trailing_taps(signal, weights):
    length = signal.shape[0]
    padded = jnp.concatenate([signal, jnp.zeros((2, signal.shape[1]), signal.dtype)], 0)
    return weights[0] * padded[0:length] + weights[1] * padded[1:length + 1] + weights[2] * padded[2:length + 2]

def reference(query_proj, key_proj, value_proj, short_taps, skip_gain, long_filter, out_grad):
    length = query_proj.shape[0]
    doubled = 2 * length
    factor_root = 1.0 / math.sqrt(length)
    query_short = causal_taps(query_proj.astype(jnp.float32), short_taps[0]).astype(jnp.bfloat16)
    key_short = causal_taps(key_proj.astype(jnp.float32), short_taps[1]).astype(jnp.bfloat16)
    value_short = causal_taps(value_proj.astype(jnp.float32), short_taps[2]).astype(jnp.bfloat16)
    key_wide = key_short.astype(jnp.float32)
    value_wide = value_short.astype(jnp.float32)
    product_in = (key_wide * value_wide).astype(jnp.bfloat16)
    kernel_own = long_filter.T * factor_root
    kernel_mirror = kernel_own[:, ::-1]
    kernel_full = jnp.concatenate([kernel_own[:1] + kernel_mirror[:1], kernel_own[1:], jnp.zeros_like(kernel_own[:1]), kernel_mirror[1:][::-1]], 0)
    spectrum_kernel = jnp.fft.rfft(kernel_full, axis=0)
    input_wide = product_in.astype(jnp.float32)
    input_spectrum = jnp.fft.rfft(input_wide, n=doubled, axis=0)
    long_mix = (jnp.fft.irfft(spectrum_kernel * input_spectrum, n=doubled, axis=0)[:length] + skip_gain * input_wide).astype(jnp.bfloat16)
    mix_wide = long_mix.astype(jnp.float32)
    query_wide = query_short.astype(jnp.float32)
    mixed_out = (query_wide * mix_wide).astype(jnp.bfloat16)
    grad_wide = out_grad.astype(jnp.float32)
    gate_grad = (grad_wide * query_wide).astype(jnp.bfloat16)
    gate_wide = gate_grad.astype(jnp.float32)
    spectrum_grad = jnp.fft.rfft(gate_wide, n=doubled, axis=0)
    input_grad = (jnp.fft.irfft(jnp.conj(spectrum_kernel) * spectrum_grad, n=doubled, axis=0)[:length] + skip_gain * gate_wide).astype(jnp.bfloat16)
    lagged = jnp.fft.irfft(jnp.conj(input_spectrum) * spectrum_grad, n=doubled, axis=0)
    reversed_part = jnp.concatenate([lagged[:1], lagged[length + 1:][::-1]], 0)
    filter_grad = ((lagged[:length] + reversed_part[:, ::-1]) * factor_root).T
    input_back = input_grad.astype(jnp.float32)
    query_grad = trailing_taps(grad_wide * mix_wide, short_taps[0]).astype(jnp.bfloat16)
    key_grad = trailing_taps(input_back * value_wide, short_taps[1]).astype(jnp.bfloat16)
    value_grad = trailing_taps(input_back * key_wide, short_taps[2]).astype(jnp.bfloat16)
    return (mixed_out, query_grad, key_grad, value_grad, filter_grad)
```

```python
import math

import jax
import jax.numpy as jnp
import ml_dtypes
import numpy as np
from jax import lax
from jax.experimental import pallas as pl
from jax.experimental.pallas import tpu as pltpu
from jax.sharding import PartitionSpec as P

F32 = jnp.float32
BF16 = jnp.bfloat16


def passed_along(array, axis, by):
    length = lax.axis_size(axis)
    pairs = [(i, i + by) for i in range(length) if 0 <= i + by < length]
    return lax.ppermute(array, axis, pairs)


def to_mirror(array):
    count = lax.axis_size("seq") * lax.axis_size("chan")
    return lax.ppermute(array, ("seq", "chan"), [(i, count - 1 - i) for i in range(count)])


def split_bf16(matrix):
    high = matrix.astype(ml_dtypes.bfloat16)
    low = (matrix - high.astype(np.float64)).astype(ml_dtypes.bfloat16)
    return high, low


def make_tables(shards, width):
    n1 = np.arange(shards)[:, None]
    k1 = np.arange(shards)[None, :] + 0.5
    n2 = np.arange(width)
    outer = 2.0 * np.pi * k1.T * n1.T / (2 * shards)
    first = np.concatenate([np.cos(outer), -np.sin(outer)], 0)
    high, low = split_bf16(first)
    first_twice = np.concatenate([high, low], 1)
    first_thrice = np.concatenate([high, low, high], 1)
    last = first.T / (shards * width)
    high, low = split_bf16(last)
    last_twice = np.concatenate([high, low], 1)
    twist = 2.0 * np.pi * k1.T * n2[None, :] / (2 * shards * width)
    twist = np.stack([np.cos(twist), np.sin(twist)]).astype(np.float32)
    inner = 2.0 * np.pi * (n2[:, None] * n2[None, :] % width) / width
    cos, sin = np.cos(inner), np.sin(inner)
    forth = np.block([[cos, -sin], [sin, cos]]).astype(ml_dtypes.bfloat16)
    forth_conj = np.block([[cos, sin], [sin, -cos]]).astype(ml_dtypes.bfloat16)
    back = np.block([[cos, sin], [-sin, cos]]).astype(ml_dtypes.bfloat16)
    back_conj = np.block([[cos, sin], [sin, -cos]]).astype(ml_dtypes.bfloat16)
    return dict(
        first_twice=first_twice,
        first_thrice=first_thrice,
        last_twice=last_twice,
        twist=twist,
        forth=forth,
        kernel_forth=np.concatenate([forth, forth_conj], 0),
        back=back,
        back_both=np.concatenate([back, back_conj], 1),
    )


def dot(left, right):
    return jnp.dot(left, right, preferred_element_type=F32)


def call(kernel, out_shape, scratch=(), flops=0, bytes_accessed=0, **more):
    return pl.pallas_call(
        kernel,
        out_shape=out_shape,
        scratch_shapes=list(scratch),
        compiler_params=pltpu.CompilerParams(vmem_limit_bytes=48 << 20),
        cost_estimate=pl.CostEstimate(
            flops=flops, bytes_accessed=bytes_accessed, transcendentals=0
        ),
        **more,
    )


def pre_kernel(q_ref, k_ref, v_ref, g_ref, halo_ref, taps_ref, qs_ref, ks_ref, vs_ref, send_ref, ext):
    rows, channels = q_ref.shape
    group = send_ref.shape[1] // 2
    for lane in range(0, channels, 128):
        lanes = pl.ds(lane, 128)
        shorts = []
        for p, ref in enumerate((q_ref, k_ref, v_ref)):
            ext[p, 0:8, :] = halo_ref[p, :, lanes]
            ext[p, 8 : rows + 8, :] = ref[:, lanes].astype(F32)
            shorts.append(
                (
                    taps_ref[p, 0:1, lanes] * ext[p, 8 : rows + 8, :]
                    + taps_ref[p, 1:2, lanes] * ext[p, 7 : rows + 7, :]
                    + taps_ref[p, 2:3, lanes] * ext[p, 6 : rows + 6, :]
                ).astype(BF16)
            )
        qs, ks, vs = shorts
        qs_ref[:, lanes] = qs
        ks_ref[:, lanes] = ks
        vs_ref[:, lanes] = vs
        product = ks.astype(F32) * vs.astype(F32)
        gate = g_ref[:, lanes].astype(F32) * qs.astype(F32)
        blocks = pl.ds(lane // group, 128 // group)
        send_ref[blocks, 0:group, :] = product.T.astype(BF16).reshape(128 // group, group, rows)
        send_ref[blocks, group:, :] = gate.T.astype(BF16).reshape(128 // group, group, rows)


def spectrum_kernel(own_ref, mir_ref, first_ref, twist_ref, forth_ref, out_ref, own_s, mir_s, lhs):
    channels, length = own_ref.shape
    shards = twist_ref.shape[1]
    width = length // shards
    scale = 1.0 / math.sqrt(length)
    for n1 in range(shards):
        own_s[n1 * channels : (n1 + 1) * channels, :] = own_ref[:, n1 * width : (n1 + 1) * width]
        mir_s[n1 * channels : (n1 + 1) * channels, :] = mir_ref[:, n1 * width : (n1 + 1) * width].astype(F32)
    cos, sin = twist_ref[0], twist_ref[1]
    step = 4

    @pl.loop(0, channels, step=step)
    def _(base):
        for i in range(step):
            c = base + i
            own = own_s[pl.ds(c, shards, stride=channels), :]
            mir = mir_s[pl.ds(channels - 1 - c, shards, stride=channels), :].astype(BF16)
            high = own.astype(BF16)
            low = (own - high.astype(F32)).astype(BF16)
            part = dot(first_ref[...], jnp.concatenate([high, high, low], 0))
            real, imag = part[:shards], part[shards:]
            rows = pl.ds(i * shards, shards)
            lhs[rows, 0:width] = (real * cos + imag * sin).astype(BF16)
            lhs[rows, width : 2 * width] = (imag * cos - real * sin).astype(BF16)
            part = dot(first_ref[:, : 2 * shards], jnp.concatenate([mir, mir], 0))
            real, imag = part[:shards], part[shards:]
            lhs[rows, 2 * width : 3 * width] = (real * cos + imag * sin).astype(BF16)
            lhs[rows, 3 * width :] = (imag * cos - real * sin).astype(BF16)
        out_ref[pl.ds(base * shards, step * shards), :] = dot(lhs[...], forth_ref[...]) * scale


def mix_kernel(x_ref, spec_ref, skip_ref, first_ref, twist_ref, forth_ref, back_ref, last_ref, out_ref, corr_ref, xs, ys, lhs, spec):
    shards, both, width = x_ref.shape
    channels = both // 2
    xs[...] = x_ref[...].reshape(shards * both, width).astype(F32)
    cos, sin = twist_ref[0], twist_ref[1]
    step = 4

    @pl.loop(0, channels, step=step)
    def _(base):
        for i in range(step):
            c = base + i
            product = xs[pl.ds(c, shards, stride=both), :].astype(BF16)
            gate = xs[pl.ds(channels + c, shards, stride=both), :].astype(BF16)
            rhs = jnp.concatenate([product, gate], 1)
            part = dot(first_ref[...], jnp.concatenate([rhs, rhs], 0))
            for j in range(2):
                real = part[:shards, j * width : (j + 1) * width]
                imag = part[shards:, j * width : (j + 1) * width]
                rows = pl.ds((2 * i + j) * shards, shards)
                lhs[rows, :width] = (real * cos + imag * sin).astype(BF16)
                lhs[rows, width:] = (imag * cos - real * sin).astype(BF16)
        spec[...] = dot(lhs[...], forth_ref[...])
        for i in range(step):
            c = base + i
            kr = spec_ref[pl.ds(c * shards, shards), :width]
            ki = spec_ref[pl.ds(c * shards, shards), width:]
            pr = spec[2 * i * shards : (2 * i + 1) * shards, :width]
            pi = spec[2 * i * shards : (2 * i + 1) * shards, width:]
            gr = spec[(2 * i + 1) * shards : (2 * i + 2) * shards, :width]
            gi = spec[(2 * i + 1) * shards : (2 * i + 2) * shards, width:]
            rows = pl.ds(2 * i * shards, shards)
            lhs[rows, :width] = (kr * pr - ki * pi).astype(BF16)
            lhs[rows, width:] = (kr * pi + ki * pr).astype(BF16)
            rows = pl.ds((2 * i + 1) * shards, shards)
            lhs[rows, :width] = (kr * gr + ki * gi).astype(BF16)
            lhs[rows, width:] = (kr * gi - ki * gr).astype(BF16)
            rows = pl.ds(c * shards, shards)
            corr_ref[rows, :width] = (pr * gr + pi * gi).astype(BF16)
            corr_ref[rows, width:] = (pr * gi - pi * gr).astype(BF16)
        spec[...] = dot(lhs[...], back_ref[...])
        for i in range(step):
            c = base + i
            columns = []
            for j in range(2):
                real = spec[(2 * i + j) * shards : (2 * i + j + 1) * shards, :width]
                imag = spec[(2 * i + j) * shards : (2 * i + j + 1) * shards, width:]
                columns.append(
                    jnp.concatenate(
                        [(real * cos - imag * sin).astype(BF16), (imag * cos + real * sin).astype(BF16)], 0
                    )
                )
            rhs = jnp.concatenate(columns, 1)
            part = dot(last_ref[...], jnp.concatenate([rhs, rhs], 0))
            skip = skip_ref[c]
            for j in range(2):
                place = pl.ds(j * channels + c, shards, stride=both)
                ys[place, :] = part[:, j * width : (j + 1) * width] + skip * xs[place, :]

    out_ref[...] = ys[...].astype(BF16).reshape(shards, both, width)


def corr_kernel(corr_ref, twist_ref, back_ref, last_ref, own_ref, mir_ref, own_s, mir_s, spec):
    channels, length = own_ref.shape
    shards = twist_ref.shape[1]
    width = length // shards
    scale = 1.0 / math.sqrt(length)
    cos, sin = twist_ref[0], twist_ref[1]
    step = 4

    @pl.loop(0, channels, step=step)
    def _(base):
        spec[...] = dot(corr_ref[pl.ds(base * shards, step * shards), :], back_ref[...])
        for i in range(step):
            c = base + i
            columns = []
            for j in range(2):
                real = spec[i * shards : (i + 1) * shards, 2 * j * width : (2 * j + 1) * width]
                imag = spec[i * shards : (i + 1) * shards, (2 * j + 1) * width : (2 * j + 2) * width]
                columns.append(
                    jnp.concatenate(
                        [(real * cos - imag * sin).astype(BF16), (imag * cos + real * sin).astype(BF16)], 0
                    )
                )
            rhs = jnp.concatenate(columns, 1)
            part = dot(last_ref[...], jnp.concatenate([rhs, rhs], 0)) * scale
            own_s[pl.ds(c, shards, stride=channels), :] = part[:, :width]
            mir_s[pl.ds(channels - 1 - c, shards, stride=channels), :] = part[:, width:]

    for n1 in range(shards):
        own_ref[:, n1 * width : (n1 + 1) * width] = own_s[n1 * channels : (n1 + 1) * channels, :]
        mir_ref[:, n1 * width : (n1 + 1) * width] = mir_s[n1 * channels : (n1 + 1) * channels, :].astype(BF16)


def head_kernel(r_ref, g_ref, ks_ref, vs_ref, out_ref):
    blocks, both, width = r_ref.shape
    group = both // 2
    channels = blocks * group
    pick = (
        lax.broadcasted_iota(jnp.int32, (8, width), 0) == lax.broadcasted_iota(jnp.int32, (8, width), 1)
    ).astype(BF16)
    across = (((1,), (1,)), ((), ()))
    mix = lax.dot_general(pick, r_ref[:, :group, :].reshape(channels, width), across, preferred_element_type=F32)
    back = lax.dot_general(pick, r_ref[:, group:, :].reshape(channels, width), across, preferred_element_type=F32)
    out_ref[0] = g_ref[0:8, :].astype(F32) * mix
    out_ref[1] = back * vs_ref[0:8, :].astype(F32)
    out_ref[2] = back * ks_ref[0:8, :].astype(F32)


def post_kernel(r_ref, g_ref, qs_ref, ks_ref, vs_ref, taps_ref, mixed_ref, q_ref, k_ref, v_ref, tail_ref, ext):
    rows, channels = g_ref.shape
    group = r_ref.shape[1] // 2
    for lane in range(0, channels, 128):
        lanes = pl.ds(lane, 128)
        blocks = pl.ds(lane // group, 128 // group)
        mix = r_ref[blocks, :group, :].reshape(128, rows).astype(F32).T
        back = r_ref[blocks, group:, :].reshape(128, rows).astype(F32).T
        mixed_ref[:, lanes] = (qs_ref[:, lanes].astype(F32) * mix).astype(BF16)
        parts = (
            g_ref[:, lanes].astype(F32) * mix,
            back * vs_ref[:, lanes].astype(F32),
            back * ks_ref[:, lanes].astype(F32),
        )
        for p, ref in enumerate((q_ref, k_ref, v_ref)):
            ext[p, 0:rows, :] = parts[p]
            tail_ref[p, :, lanes] = parts[p][rows - 16 :]
            ref[:, lanes] = (
                taps_ref[p, 0:1, lanes] * parts[p]
                + taps_ref[p, 1:2, lanes] * ext[p, 1 : rows + 1, :]
                + taps_ref[p, 2:3, lanes] * ext[p, 2 : rows + 2, :]
            ).astype(BF16)


def tail_kernel(tail_ref, halo_ref, taps_ref, q_in, k_in, v_in, q_ref, k_ref, v_ref, ext):
    for p, ref in enumerate((q_ref, k_ref, v_ref)):
        ext[0:16, :] = tail_ref[p]
        ext[16:24, :] = halo_ref[p]
        ref[...] = (
            taps_ref[p, 0:1, :] * ext[0:16, :]
            + taps_ref[p, 1:2, :] * ext[1:17, :]
            + taps_ref[p, 2:3, :] * ext[2:18, :]
        ).astype(BF16)


def per_device(query_proj, key_proj, value_proj, short_taps, skip_gain, long_filter, out_grad):
    positions, width = query_proj.shape
    channels, length = long_filter.shape
    shards = lax.axis_size("seq")
    tables = make_tables(shards, positions)
    shape = jax.ShapeDtypeStruct
    own_skip = lax.dynamic_slice_in_dim(skip_gain, lax.axis_index("seq") * channels, channels)

    filter_far = to_mirror(long_filter.astype(BF16))

    ends = jnp.stack([x[positions - 2 :] for x in (query_proj, key_proj, value_proj)])
    previous = passed_along(ends, "seq", 1).astype(F32)
    previous = jnp.pad(previous, ((0, 0), (6, 0), (0, 0)))
    wide = shape((positions, width), BF16)
    query_short, key_short, value_short, send = call(
        pre_kernel,
        (wide, wide, wide, shape((shards, 2 * channels, positions), BF16)),
        [pltpu.VMEM((3, positions + 8, 128), F32)],
        flops=30 * positions * width,
        bytes_accessed=18 * positions * width,
    )(query_proj, key_proj, value_proj, out_grad, previous, short_taps)
    received = lax.all_to_all(send, "seq", split_axis=0, concat_axis=0, tiled=True)

    step = 4
    spectrum = call(
        spectrum_kernel,
        shape((channels * shards, 2 * positions), F32),
        [
            pltpu.VMEM((shards * channels, positions), F32),
            pltpu.VMEM((shards * channels, positions), F32),
            pltpu.VMEM((step * shards, 4 * positions), BF16),
        ],
        flops=16 * 2 * channels * shards * positions * positions,
        bytes_accessed=14 * channels * length,
    )(long_filter, filter_far, tables["first_thrice"], tables["twist"], tables["kernel_forth"])

    returned, corr = call(
        mix_kernel,
        (
            shape((shards, 2 * channels, positions), BF16),
            shape((channels * shards, 2 * positions), BF16),
        ),
        [
            pltpu.VMEM((shards * 2 * channels, positions), F32),
            pltpu.VMEM((shards * 2 * channels, positions), F32),
            pltpu.VMEM((2 * step * shards, 2 * positions), BF16),
            pltpu.VMEM((2 * step * shards, 2 * positions), F32),
        ],
        flops=32 * 2 * channels * shards * positions * positions,
        bytes_accessed=24 * channels * length,
        in_specs=[pl.BlockSpec(memory_space=pltpu.VMEM)] * 2
        + [pl.BlockSpec(memory_space=pltpu.SMEM)]
        + [pl.BlockSpec(memory_space=pltpu.VMEM)] * 5,
    )(
        received,
        spectrum,
        own_skip,
        tables["first_twice"],
        tables["twist"],
        tables["forth"],
        tables["back"],
        tables["last_twice"],
    )
    result = lax.all_to_all(returned, "seq", split_axis=0, concat_axis=0, tiled=True)

    lagged, lagged_back = call(
        corr_kernel,
        (shape((channels, length), F32), shape((channels, length), BF16)),
        [
            pltpu.VMEM((shards * channels, positions), F32),
            pltpu.VMEM((shards * channels, positions), F32),
            pltpu.VMEM((step * shards, 4 * positions), F32),
        ],
        flops=16 * 2 * channels * shards * positions * positions,
        bytes_accessed=12 * channels * length,
    )(corr, tables["twist"], tables["back_both"], tables["last_twice"])
    filter_grad = lagged + to_mirror(lagged_back).astype(F32)

    head = call(
        head_kernel,
        shape((3, 8, width), F32),
        flops=64 * positions * width,
        bytes_accessed=4 * positions * width,
    )(result, out_grad, key_short, value_short)
    following = passed_along(head, "seq", -1)
    mixed_out, query_part, key_part, value_part, tail = call(
        post_kernel,
        (wide, wide, wide, wide, shape((3, 16, width), F32)),
        [pltpu.VMEM((3, positions + 8, 128), F32)],
        flops=30 * positions * width,
        bytes_accessed=20 * positions * width,
    )(result, out_grad, query_short, key_short, value_short, short_taps)
    last = pl.BlockSpec((16, width), lambda i: (positions // 16 - 1, 0))
    whole = lambda *dims: pl.BlockSpec(dims, lambda i: (0,) * len(dims))
    query_grad, key_grad, value_grad = call(
        tail_kernel,
        (wide, wide, wide),
        [pltpu.VMEM((24, width), F32)],
        flops=30 * 16 * width,
        bytes_accessed=30 * 16 * width,
        grid=(1,),
        in_specs=[whole(3, 16, width), whole(3, 8, width), whole(3, 3, width), last, last, last],
        out_specs=[last, last, last],
        input_output_aliases={3: 0, 4: 1, 5: 2},
    )(tail, following, short_taps, query_part, key_part, value_part)
    return (mixed_out, query_grad, key_grad, value_grad, filter_grad)


def solution(mesh):
    in_specs = (
        P("seq", "chan"),
        P("seq", "chan"),
        P("seq", "chan"),
        P(None, None, "chan"),
        P("chan"),
        P(("chan", "seq"), None),
        P("seq", "chan"),
    )
    out_specs = (
        P("seq", "chan"),
        P("seq", "chan"),
        P("seq", "chan"),
        P("seq", "chan"),
        P(("chan", "seq"), None),
    )
    return jax.shard_map(
        per_device, mesh=mesh, in_specs=in_specs, out_specs=out_specs, check_vma=False
    )
```

```python
import math

import jax
import jax.numpy as jnp
import ml_dtypes
import numpy as np
from jax import lax
from jax.experimental import pallas as pl
from jax.experimental.pallas import tpu as pltpu
from jax.sharding import PartitionSpec as P

F32 = jnp.float32
BF16 = jnp.bfloat16

SPEC_FLOPS = 1 << 34
CORR_FLOPS = 1 << 29
MIX_FLOPS = 1 << 29
ADD_FLOPS = 1 << 34


def passed_along(array, axis, by):
    length = lax.axis_size(axis)
    pairs = [(i, i + by) for i in range(length) if 0 <= i + by < length]
    return lax.ppermute(array, axis, pairs)


def to_mirror(array):
    count = lax.axis_size("seq") * lax.axis_size("chan")
    return lax.ppermute(array, ("seq", "chan"), [(i, count - 1 - i) for i in range(count)])


def split_bf16(matrix):
    high = matrix.astype(ml_dtypes.bfloat16)
    low = (matrix - high.astype(np.float64)).astype(ml_dtypes.bfloat16)
    return high, low


def make_tables(shards, width):
    n1 = np.arange(shards)[:, None]
    k1 = np.arange(shards)[None, :] + 0.5
    n2 = np.arange(width)
    outer = 2.0 * np.pi * k1.T * n1.T / (2 * shards)
    first = np.concatenate([np.cos(outer), -np.sin(outer)], 0)
    high, low = split_bf16(first)
    first_thrice = np.concatenate([high, low, high], 1)
    last = first.T / (shards * width)
    high, low = split_bf16(last)
    last_twice = np.concatenate([high, low], 1)
    twist = 2.0 * np.pi * k1.T * n2[None, :] / (2 * shards * width)
    twist = np.stack([np.cos(twist), np.sin(twist)]).astype(np.float32)
    inner = 2.0 * np.pi * (n2[:, None] * n2[None, :] % width) / width
    cos, sin = np.cos(inner), np.sin(inner)
    forth = np.block([[cos, -sin], [sin, cos]])
    conj = np.block([[cos, sin], [sin, -cos]])
    back = np.block([[cos, sin], [-sin, cos]])
    square = np.concatenate([forth, conj, back], 0).astype(ml_dtypes.bfloat16)
    first_thrice = np.pad(first_thrice, ((0, 0), (0, 2 * width - 3 * shards)))
    return np.concatenate([square, first_thrice, last_twice], 0), twist


def table_views(table_ref, shards, width):
    at = 6 * width
    return dict(
        forth=table_ref.at[0 : 2 * width],
        kernel_forth=table_ref.at[0 : 4 * width],
        conj=table_ref.at[2 * width : 4 * width],
        back=table_ref.at[4 * width : at],
        first_twice=table_ref.at[at : at + 2 * shards, : 2 * shards],
        first_thrice=table_ref.at[at : at + 2 * shards, : 3 * shards],
        last_twice=table_ref.at[at + 2 * shards : at + 3 * shards, :],
    )


def dot(left, right):
    return jnp.dot(left, right, preferred_element_type=F32)


def call(kernel, out_shape, scratch=(), flops=0, bytes_accessed=0, limit=44, **more):
    return pl.pallas_call(
        kernel,
        out_shape=out_shape,
        scratch_shapes=list(scratch),
        compiler_params=pltpu.CompilerParams(vmem_limit_bytes=limit << 20),
        cost_estimate=pl.CostEstimate(
            flops=flops, bytes_accessed=bytes_accessed, transcendentals=0
        ),
        **more,
    )


def ends_kernel(q_hbm, k_hbm, v_hbm, g_hbm, last_ref, first_ref, held, sems):
    rows = q_hbm.shape[0]
    sources = [ref.at[rows - 16 :] for ref in (q_hbm, k_hbm, v_hbm)] + [ref.at[:16] for ref in (g_hbm, k_hbm, v_hbm)]
    copies = [pltpu.make_async_copy(src, held.at[p], sems.at[p]) for p, src in enumerate(sources)]
    for copy in copies:
        copy.start()
    for p, copy in enumerate(copies):
        copy.wait()
        if p < 3:
            last_ref[p] = held[p].astype(F32)[14:16].astype(BF16)
        else:
            first_ref[p - 3] = held[p].astype(F32)[0:2].astype(BF16)


def pre_kernel(q_hbm, k_hbm, v_hbm, g_hbm, halo_ref, taps_ref, qs_ref, ks_ref, vs_ref, send_ref, ends_ref, q_ref, k_ref, v_ref, g_ref, ext, sems):
    copies = [
        pltpu.make_async_copy(src, dst, sems.at[p])
        for p, (src, dst) in enumerate(((q_hbm, q_ref), (k_hbm, k_ref), (v_hbm, v_ref), (g_hbm, g_ref)))
    ]
    for copy in copies:
        copy.start()
    for copy in copies:
        copy.wait()
    rows, channels = q_ref.shape
    group = send_ref.shape[1] // 2
    for lane in range(0, channels, 128):
        lanes = pl.ds(lane, 128)
        shorts = []
        for p, ref in enumerate((q_ref, k_ref, v_ref)):
            ext[p, 6:8, :] = halo_ref[p, :, lanes].astype(F32)
            ext[p, 8 : rows + 8, :] = ref[:, lanes].astype(F32)
            shorts.append(
                (
                    taps_ref[p, 0:1, lanes] * ext[p, 8 : rows + 8, :]
                    + taps_ref[p, 1:2, lanes] * ext[p, 7 : rows + 7, :]
                    + taps_ref[p, 2:3, lanes] * ext[p, 6 : rows + 6, :]
                ).astype(BF16)
            )
        qs, ks, vs = shorts
        qs_ref[:, lanes] = qs
        ks_ref[:, lanes] = ks
        vs_ref[:, lanes] = vs
        product = ks.astype(F32) * vs.astype(F32)
        gate = g_ref[:, lanes].astype(F32) * qs.astype(F32)
        for p in (1, 2):
            ends_ref[p - 1, :, lanes] = ext[p, rows + 6 : rows + 8, :].astype(BF16)
        blocks = pl.ds(lane // group, 128 // group)
        send_ref[blocks, 0:group, :] = product.T.astype(BF16).reshape(128 // group, group, rows)
        send_ref[blocks, group:, :] = gate.T.astype(BF16).reshape(128 // group, group, rows)


def spectrum_kernel(own_ref, mir_ref, skip_ref, table_ref, twist_ref, out_ref, own_s, mir_s, lhs):
    channels, length = own_ref.shape
    shards = twist_ref.shape[1]
    width = length // shards
    table = table_views(table_ref, shards, width)
    first_ref, forth_ref = table["first_thrice"], table["kernel_forth"]
    scale = 1.0 / math.sqrt(length)
    first_channel = lax.axis_index("seq") * channels
    for n1 in range(shards):
        own_s[n1 * channels : (n1 + 1) * channels, :] = own_ref[:, n1 * width : (n1 + 1) * width]
        mir_s[n1 * channels : (n1 + 1) * channels, :] = mir_ref[:, n1 * width : (n1 + 1) * width].astype(F32)
    cos, sin = twist_ref[0], twist_ref[1]
    step = 4

    @pl.loop(0, channels, step=step)
    def _(base):
        for i in range(step):
            c = base + i
            own = own_s[pl.ds(c, shards, stride=channels), :]
            mir = mir_s[pl.ds(channels - 1 - c, shards, stride=channels), :].astype(BF16)
            high = own.astype(BF16)
            low = (own - high.astype(F32)).astype(BF16)
            part = dot(first_ref[...], jnp.concatenate([high, high, low], 0))
            real, imag = part[:shards], part[shards:]
            rows = pl.ds(i * shards, shards)
            lhs[rows, 0:width] = (real * cos + imag * sin).astype(BF16)
            lhs[rows, width : 2 * width] = (imag * cos - real * sin).astype(BF16)
            part = dot(table["first_twice"][...], jnp.concatenate([mir, mir], 0))
            real, imag = part[:shards], part[shards:]
            lhs[rows, 2 * width : 3 * width] = (real * cos + imag * sin).astype(BF16)
            lhs[rows, 3 * width :] = (imag * cos - real * sin).astype(BF16)
        part = dot(lhs[...], forth_ref[...]) * scale
        for i in range(step):
            c = base + i
            rows = pl.ds(c * shards, shards)
            out_ref[rows, :width] = part[i * shards : (i + 1) * shards, :width] + skip_ref[first_channel + c]
            out_ref[rows, width:] = part[i * shards : (i + 1) * shards, width:]


def signals_from(spec, shards, width, cos, sin, last_ref):
    columns = []
    for real, imag in spec:
        columns.append(
            jnp.concatenate([(real * cos - imag * sin).astype(BF16), (imag * cos + real * sin).astype(BF16)], 0)
        )
    rhs = jnp.concatenate(columns, 1)
    return dot(last_ref[...], jnp.concatenate([rhs, rhs], 0))


def corr_kernel(x_ref, table_ref, twist_ref, spectra_ref, own_ref, mir_ref, xs, own_s, mir_s, lhs, spec):
    shards, both, width = x_ref.shape
    channels = both // 2
    table = table_views(table_ref, shards, width)
    first_ref, last_ref = table["first_twice"], table["last_twice"]
    scale = 1.0 / math.sqrt(shards * width)
    xs[...] = x_ref[...].reshape(shards * both, width).astype(F32)
    cos, sin = twist_ref[0], twist_ref[1]
    step = 4

    @pl.loop(0, channels, step=step)
    def _(base):
        for i in range(step):
            c = base + i
            product = xs[pl.ds(c, shards, stride=both), :].astype(BF16)
            gate = xs[pl.ds(channels + c, shards, stride=both), :].astype(BF16)
            rhs = jnp.concatenate([product, gate], 1)
            part = dot(first_ref[...], jnp.concatenate([rhs, rhs], 0))
            for j in range(2):
                real = part[:shards, j * width : (j + 1) * width]
                imag = part[shards:, j * width : (j + 1) * width]
                rows = pl.ds((2 * i + j) * shards, shards)
                lhs[rows, :width] = (real * cos + imag * sin).astype(BF16)
                lhs[rows, width:] = (imag * cos - real * sin).astype(BF16)
        both_spec = dot(lhs[...], table["forth"][...])
        spectra_ref[pl.ds(2 * base * shards, 2 * step * shards), :] = both_spec
        for i in range(step):
            pr = both_spec[2 * i * shards : (2 * i + 1) * shards, :width]
            pi = both_spec[2 * i * shards : (2 * i + 1) * shards, width:]
            gr = both_spec[(2 * i + 1) * shards : (2 * i + 2) * shards, :width]
            gi = both_spec[(2 * i + 1) * shards : (2 * i + 2) * shards, width:]
            rows = pl.ds(i * shards, shards)
            lhs[rows, :width] = (pr * gr + pi * gi).astype(BF16)
            lhs[rows, width:] = (pr * gi - pi * gr).astype(BF16)
        product = lhs[: step * shards, :]
        spec[:, : 2 * width] = dot(product, table["back"][...])
        spec[:, 2 * width :] = dot(product, table["conj"][...])
        for i in range(step):
            c = base + i
            rows = slice(i * shards, (i + 1) * shards)
            pairs = [
                (spec[rows, 2 * j * width : (2 * j + 1) * width], spec[rows, (2 * j + 1) * width : (2 * j + 2) * width])
                for j in range(2)
            ]
            part = signals_from(pairs, shards, width, cos, sin, last_ref) * scale
            own_s[pl.ds(c, shards, stride=channels), :] = part[:, :width]
            mir_s[pl.ds(channels - 1 - c, shards, stride=channels), :] = part[:, width:]

    for n1 in range(shards):
        own_ref[:, n1 * width : (n1 + 1) * width] = own_s[n1 * channels : (n1 + 1) * channels, :]
        mir_ref[:, n1 * width : (n1 + 1) * width] = mir_s[n1 * channels : (n1 + 1) * channels, :].astype(BF16)


def mix_kernel(spectra_ref, spec_ref, table_ref, twist_ref, out_ref, ys, lhs, spec, first_s, extra_s):
    shards, rows_sent, width = out_ref.shape
    channels = spec_ref.shape[0] // shards
    both = 2 * channels
    table = table_views(table_ref, shards, width)
    last_ref = table["last_twice"]
    cos, sin = twist_ref[0], twist_ref[1]
    step = 4
    lane_channel = lax.broadcasted_iota(jnp.int32, (shards, width), 1) % channels
    first_s[...] = jnp.zeros_like(first_s)

    @pl.loop(0, channels, step=step)
    def _(base):
        for i in range(step):
            c = base + i
            kr = spec_ref[pl.ds(c * shards, shards), :width]
            ki = spec_ref[pl.ds(c * shards, shards), width:]
            pr = spectra_ref[pl.ds(2 * c * shards, shards), :width]
            pi = spectra_ref[pl.ds(2 * c * shards, shards), width:]
            gr = spectra_ref[pl.ds((2 * c + 1) * shards, shards), :width]
            gi = spectra_ref[pl.ds((2 * c + 1) * shards, shards), width:]
            rows = pl.ds(2 * i * shards, shards)
            lhs[rows, :width] = (kr * pr - ki * pi).astype(BF16)
            lhs[rows, width:] = (kr * pi + ki * pr).astype(BF16)
            rows = pl.ds((2 * i + 1) * shards, shards)
            lhs[rows, :width] = (kr * gr + ki * gi).astype(BF16)
            lhs[rows, width:] = (kr * gi - ki * gr).astype(BF16)
        spec[...] = dot(lhs[...], table["back"][...])
        firsts = [jnp.zeros((shards, width), F32)] * 4
        for i in range(step):
            c = base + i
            pairs = []
            for j in range(2):
                rows = slice((2 * i + j) * shards, (2 * i + j + 1) * shards)
                pairs.append((spec[rows, :width], spec[rows, width:]))
            part = signals_from(pairs, shards, width, cos, sin, last_ref)
            for j in range(2):
                ys[pl.ds(j * channels + c, shards, stride=both), :] = part[:, j * width : (j + 1) * width]
                for p in range(2):
                    column = jnp.broadcast_to(part[:, j * width + p : j * width + p + 1], (shards, width))
                    firsts[2 * j + p] = jnp.where(lane_channel == c, column, firsts[2 * j + p])
        for k in range(4):
            first_s[k, :shards, :] += firsts[k]

    out_ref[:, :both, :] = ys[...].astype(BF16).reshape(shards, both, width)
    extra_s[...] = jnp.zeros_like(extra_s)
    for k in range(4):
        extra_s[pl.ds(k, shards, stride=8), :] = first_s[k, 1 : shards + 1, :]
    out_ref[:, both:, :] = extra_s[...].astype(BF16).reshape(shards, 8, width)


def post_kernel(r_ref, g_ref, qs_ref, ks_ref, vs_ref, ends_ref, next_ref, taps_ref, mixed_ref, q_ref, k_ref, v_ref, ext, around):
    rows, channels = g_ref.shape
    group = (r_ref.shape[1] - 8) // 2
    count = 128 // group
    shape = (count, 8, 128)
    mine = lax.broadcasted_iota(jnp.int32, shape, 2) // group == lax.broadcasted_iota(jnp.int32, shape, 0)
    for lane in range(0, channels, 128):
        lanes = pl.ds(lane, 128)
        blocks = pl.ds(lane // group, count)
        mix = r_ref[blocks, :group, :].reshape(128, rows).astype(F32).T
        back = r_ref[blocks, group : 2 * group, :].reshape(128, rows).astype(F32).T
        beyond = jnp.sum(jnp.where(mine, r_ref[blocks, 2 * group :, :].astype(F32), 0.0), 0)
        mixed_ref[:, lanes] = (qs_ref[:, lanes].astype(F32) * mix).astype(BF16)
        near = (g_ref, ks_ref, vs_ref)
        gate, key, value = [ref[:, lanes].astype(F32) for ref in near]
        gate_next = next_ref[0, :, lanes].astype(F32)
        shorts_next = []
        for p in (1, 2):
            around[0:2, :] = ends_ref[p - 1, :, lanes].astype(F32)
            around[2:4, :] = next_ref[p, :, lanes].astype(F32)
            shorts_next.append(
                (
                    taps_ref[p, 0:1, lanes] * around[2:4, :]
                    + taps_ref[p, 1:2, lanes] * around[1:3, :]
                    + taps_ref[p, 2:3, lanes] * around[0:2, :]
                )
                .astype(BF16)
                .astype(F32)
            )
        key_next, value_next = shorts_next
        parts = (gate * mix, back * value, back * key)
        beyonds = (gate_next * beyond[0:2], beyond[2:4] * value_next, beyond[2:4] * key_next)
        for p, ref in enumerate((q_ref, k_ref, v_ref)):
            ext[p, 0:rows, :] = parts[p]
            ext[p, rows : rows + 2, :] = beyonds[p]
            ref[:, lanes] = (
                taps_ref[p, 0:1, lanes] * parts[p]
                + taps_ref[p, 1:2, lanes] * ext[p, 1 : rows + 1, :]
                + taps_ref[p, 2:3, lanes] * ext[p, 2 : rows + 2, :]
            ).astype(BF16)


def add_kernel(near_ref, far_ref, out_ref):
    out_ref[...] = near_ref[...] + far_ref[...].astype(F32)


def per_device(query_proj, key_proj, value_proj, short_taps, skip_gain, long_filter, out_grad):
    positions, width = query_proj.shape
    channels, length = long_filter.shape
    shards = lax.axis_size("seq")
    table, twist = make_tables(shards, positions)
    shape = jax.ShapeDtypeStruct

    near = [pltpu.with_memory_space_constraint(x, pltpu.HBM) for x in (query_proj, key_proj, value_proj, out_grad)]
    ends, starts = call(
        ends_kernel,
        (shape((3, 2, width), BF16), shape((3, 2, width), BF16)),
        [pltpu.VMEM((6, 16, width), BF16), pltpu.SemaphoreType.DMA((6,))],
        bytes_accessed=200 * width,
        in_specs=[pl.BlockSpec(memory_space=pltpu.HBM)] * 4,
    )(*near)
    previous = passed_along(ends, "seq", 1)
    previous, filter_sent = lax.optimization_barrier((previous, long_filter.astype(BF16)))
    filter_far = to_mirror(filter_sent)
    wide = shape((positions, width), BF16)
    query_short, key_short, value_short, send, own_ends = call(
        pre_kernel,
        (wide, wide, wide, shape((shards, 2 * channels, positions), BF16), shape((2, 2, width), BF16)),
        [
            *[pltpu.VMEM((positions, width), BF16)] * 4,
            pltpu.VMEM((3, positions + 8, 128), F32),
            pltpu.SemaphoreType.DMA((4,)),
        ],
        flops=30 * positions * width,
        bytes_accessed=18 * positions * width,
        in_specs=[pl.BlockSpec(memory_space=pltpu.HBM)] * 4
        + [pl.BlockSpec(memory_space=pltpu.VMEM)] * 2,
    )(*near, previous, short_taps)
    received = lax.all_to_all(send, "seq", split_axis=0, concat_axis=0, tiled=True)

    step = 4
    spectrum = call(
        spectrum_kernel,
        shape((channels * shards, 2 * positions), F32),
        [
            pltpu.VMEM((shards * channels, positions), F32),
            pltpu.VMEM((shards * channels, positions), F32),
            pltpu.VMEM((step * shards, 4 * positions), BF16),
        ],
        flops=SPEC_FLOPS,
        bytes_accessed=14 * channels * length,
        in_specs=[pl.BlockSpec(memory_space=pltpu.VMEM)] * 2
        + [pl.BlockSpec(memory_space=pltpu.SMEM)]
        + [pl.BlockSpec(memory_space=pltpu.VMEM)] * 2,
    )(long_filter, filter_far, skip_gain, table, twist)

    received, spectrum = lax.optimization_barrier((received, spectrum))
    spectra, lagged, lagged_back = call(
        corr_kernel,
        (
            shape((2 * channels * shards, 2 * positions), F32),
            shape((channels, length), F32),
            shape((channels, length), BF16),
        ),
        [
            pltpu.VMEM((shards * 2 * channels, positions), F32),
            pltpu.VMEM((shards * channels, positions), F32),
            pltpu.VMEM((shards * channels, positions), F32),
            pltpu.VMEM((2 * step * shards, 2 * positions), BF16),
            pltpu.VMEM((step * shards, 4 * positions), F32),
        ],
        flops=CORR_FLOPS,
        bytes_accessed=24 * channels * length,
    )(received, table, twist)
    lagged_far = to_mirror(lagged_back)

    returned = call(
        mix_kernel,
        shape((shards, 2 * channels + 8, positions), BF16),
        [
            pltpu.VMEM((shards * 2 * channels, positions), F32),
            pltpu.VMEM((2 * step * shards, 2 * positions), BF16),
            pltpu.VMEM((2 * step * shards, 2 * positions), F32),
            pltpu.VMEM((4, shards + 8, positions), F32),
            pltpu.VMEM((shards * 8, positions), F32),
        ],
        flops=MIX_FLOPS,
        bytes_accessed=24 * channels * length,
    )(spectra, spectrum, table, twist)
    result = lax.all_to_all(returned, "seq", split_axis=0, concat_axis=0, tiled=True)

    filter_grad = call(
        add_kernel,
        shape((channels, length), F32),
        flops=ADD_FLOPS,
        bytes_accessed=10 * channels * length,
    )(lagged, lagged_far)
    starts, filter_grad = lax.optimization_barrier((starts, filter_grad))
    following = passed_along(starts, "seq", -1)
    mixed_out, query_grad, key_grad, value_grad = call(
        post_kernel,
        (wide, wide, wide, wide),
        [pltpu.VMEM((3, positions + 8, 128), F32), pltpu.VMEM((8, 128), F32)],
        flops=30 * positions * width,
        bytes_accessed=20 * positions * width,
    )(result, out_grad, query_short, key_short, value_short, own_ends, following, short_taps)
    return (mixed_out, query_grad, key_grad, value_grad, filter_grad)


def solution(mesh):
    in_specs = (
        P("seq", "chan"),
        P("seq", "chan"),
        P("seq", "chan"),
        P(None, None, "chan"),
        P("chan"),
        P(("chan", "seq"), None),
        P("seq", "chan"),
    )
    out_specs = (
        P("seq", "chan"),
        P("seq", "chan"),
        P("seq", "chan"),
        P("seq", "chan"),
        P(("chan", "seq"), None),
    )
    return jax.shard_map(
        per_device, mesh=mesh, in_specs=in_specs, out_specs=out_specs, check_vma=False
    )
```

```python
import math

import jax
import jax.numpy as jnp
import ml_dtypes
import numpy as np
from jax import lax
from jax.experimental import pallas as pl
from jax.experimental.pallas import tpu as pltpu
from jax.sharding import PartitionSpec as P

F32 = jnp.float32
BF16 = jnp.bfloat16

SPEC_FLOPS = 1 << 34
CORR_FLOPS = 1 << 29
MIX_FLOPS = 1 << 29
ADD_FLOPS = 1 << 34


def passed_along(array, axis, by):
    length = lax.axis_size(axis)
    pairs = [(i, i + by) for i in range(length) if 0 <= i + by < length]
    return lax.ppermute(array, axis, pairs)


def to_mirror(array):
    count = lax.axis_size("seq") * lax.axis_size("chan")
    return lax.ppermute(array, ("seq", "chan"), [(i, count - 1 - i) for i in range(count)])


def split_bf16(matrix):
    high = matrix.astype(ml_dtypes.bfloat16)
    low = (matrix - high.astype(np.float64)).astype(ml_dtypes.bfloat16)
    return high, low


def make_tables(shards, width):
    n1 = np.arange(shards)[:, None]
    k1 = np.arange(shards)[None, :] + 0.5
    n2 = np.arange(width)
    outer = 2.0 * np.pi * k1.T * n1.T / (2 * shards)
    first = np.concatenate([np.cos(outer), -np.sin(outer)], 0)
    high, low = split_bf16(first)
    first_thrice = np.concatenate([high, low, high], 1)
    last = first.T / (shards * width)
    high, low = split_bf16(last)
    last_twice = np.pad(np.concatenate([high, low], 0), ((0, 0), (0, 2 * width - 2 * shards)))
    twist = 2.0 * np.pi * k1.T * n2[None, :] / (2 * shards * width)
    twist = np.stack([np.cos(twist), np.sin(twist)]).astype(np.float32)
    inner = 2.0 * np.pi * (n2[:, None] * n2[None, :] % width) / width
    cos, sin = np.cos(inner), np.sin(inner)
    forth = np.block([[cos, -sin], [sin, cos]])
    conj = np.block([[cos, sin], [sin, -cos]])
    back = np.block([[cos, sin], [-sin, cos]])
    square = np.concatenate([forth, conj, back], 0).astype(ml_dtypes.bfloat16)
    first_thrice = np.pad(first_thrice, ((0, 0), (0, 2 * width - 3 * shards)))
    return np.concatenate([square, first_thrice, last_twice], 0), twist


def table_views(table_ref, shards, width):
    at = 6 * width
    return dict(
        forth=table_ref.at[0 : 2 * width],
        kernel_forth=table_ref.at[0 : 4 * width],
        conj=table_ref.at[2 * width : 4 * width],
        back=table_ref.at[4 * width : at],
        first_twice=table_ref.at[at : at + 2 * shards, : 2 * shards],
        first_thrice=table_ref.at[at : at + 2 * shards, : 3 * shards],
        last_twice=table_ref.at[at + 2 * shards : at + 4 * shards, : 2 * shards],
    )


def dot(left, right):
    return jnp.dot(left, right, preferred_element_type=F32)


def call(kernel, out_shape, scratch=(), flops=0, bytes_accessed=0, limit=44, **more):
    return pl.pallas_call(
        kernel,
        out_shape=out_shape,
        scratch_shapes=list(scratch),
        compiler_params=pltpu.CompilerParams(vmem_limit_bytes=limit << 20),
        cost_estimate=pl.CostEstimate(
            flops=flops, bytes_accessed=bytes_accessed, transcendentals=0
        ),
        **more,
    )


def ends_kernel(q_hbm, k_hbm, v_hbm, g_hbm, last_ref, first_ref, held, sems):
    rows = q_hbm.shape[0]
    sources = [ref.at[rows - 16 :] for ref in (q_hbm, k_hbm, v_hbm)] + [ref.at[:16] for ref in (g_hbm, k_hbm, v_hbm)]
    copies = [pltpu.make_async_copy(src, held.at[p], sems.at[p]) for p, src in enumerate(sources)]
    for copy in copies:
        copy.start()
    for p, copy in enumerate(copies):
        copy.wait()
        if p < 3:
            last_ref[p] = held[p].astype(F32)[14:16].astype(BF16)
        else:
            first_ref[p - 3] = held[p].astype(F32)[0:2].astype(BF16)


def pre_kernel(
    q_hbm, k_hbm, v_hbm, g_hbm, taps_hbm, halo_ref, qs_ref, ks_ref, vs_ref, send_hbm, ends_ref, q_ref, k_ref, v_ref, g_ref, taps_ref, send_ref, ext, sems, out_sems
):
    rows, channels = q_ref.shape
    group = send_ref.shape[1] // 2
    chunks = sems.shape[0]
    size = channels // chunks
    taps_copy = pltpu.make_async_copy(taps_hbm, taps_ref, out_sems.at[chunks])
    taps_copy.start()
    pairs = ((q_hbm, q_ref), (k_hbm, k_ref), (v_hbm, v_ref), (g_hbm, g_ref))
    copies = []
    for chunk in range(chunks):
        lanes = pl.ds(chunk * size, size)
        copies.append(
            [pltpu.make_async_copy(src.at[:, lanes], dst.at[:, lanes], sems.at[chunk, p]) for p, (src, dst) in enumerate(pairs)]
        )
        for copy in copies[-1]:
            copy.start()
    taps_copy.wait()
    sends = []
    for chunk in range(chunks):
        for copy in copies[chunk]:
            copy.wait()
        for lane in range(chunk * size, (chunk + 1) * size, 128):
            lanes = pl.ds(lane, 128)
            shorts = []
            for p, ref in enumerate((q_ref, k_ref, v_ref)):
                ext[p, 6:8, :] = halo_ref[p, :, lanes].astype(F32)
                ext[p, 8 : rows + 8, :] = ref[:, lanes].astype(F32)
                shorts.append(
                    (
                        taps_ref[p, 0:1, lanes] * ext[p, 8 : rows + 8, :]
                        + taps_ref[p, 1:2, lanes] * ext[p, 7 : rows + 7, :]
                        + taps_ref[p, 2:3, lanes] * ext[p, 6 : rows + 6, :]
                    ).astype(BF16)
                )
            qs, ks, vs = shorts
            qs_ref[:, lanes] = qs
            ks_ref[:, lanes] = ks
            vs_ref[:, lanes] = vs
            product = ks.astype(F32) * vs.astype(F32)
            gate = g_ref[:, lanes].astype(F32) * qs.astype(F32)
            for p in (1, 2):
                ends_ref[p - 1, :, lanes] = ext[p, rows + 6 : rows + 8, :].astype(BF16)
            blocks = pl.ds(lane // group, 128 // group)
            send_ref[blocks, 0:group, :] = product.T.astype(BF16).reshape(128 // group, group, rows)
            send_ref[blocks, group:, :] = gate.T.astype(BF16).reshape(128 // group, group, rows)
        blocks = pl.ds(chunk * size // group, size // group)
        sends.append(pltpu.make_async_copy(send_ref.at[blocks], send_hbm.at[blocks], out_sems.at[chunk]))
        sends[-1].start()
    for copy in sends:
        copy.wait()


def spectrum_kernel(own_ref, mir_ref, skip_ref, table_ref, twist_ref, out_ref, own_s, mir_s, lhs):
    channels, length = own_ref.shape
    shards = twist_ref.shape[1]
    width = length // shards
    table = table_views(table_ref, shards, width)
    first_ref, forth_ref = table["first_thrice"], table["kernel_forth"]
    scale = 1.0 / math.sqrt(length)
    first_channel = lax.axis_index("seq") * channels
    for n1 in range(shards):
        own_s[n1 * channels : (n1 + 1) * channels, :] = own_ref[:, n1 * width : (n1 + 1) * width]
        mir_s[n1 * channels : (n1 + 1) * channels, :] = mir_ref[:, n1 * width : (n1 + 1) * width].astype(F32)
    cos, sin = twist_ref[0], twist_ref[1]
    step = 4

    @pl.loop(0, channels, step=step)
    def _(base):
        for i in range(step):
            c = base + i
            own = own_s[pl.ds(c, shards, stride=channels), :]
            mir = mir_s[pl.ds(channels - 1 - c, shards, stride=channels), :].astype(BF16)
            high = own.astype(BF16)
            low = (own - high.astype(F32)).astype(BF16)
            part = dot(first_ref[...], jnp.concatenate([high, high, low], 0))
            real, imag = part[:shards], part[shards:]
            rows = pl.ds(i * shards, shards)
            lhs[rows, 0:width] = (real * cos + imag * sin).astype(BF16)
            lhs[rows, width : 2 * width] = (imag * cos - real * sin).astype(BF16)
            part = dot(table["first_twice"][...], jnp.concatenate([mir, mir], 0))
            real, imag = part[:shards], part[shards:]
            lhs[rows, 2 * width : 3 * width] = (real * cos + imag * sin).astype(BF16)
            lhs[rows, 3 * width :] = (imag * cos - real * sin).astype(BF16)
        part = dot(lhs[...], forth_ref[...]) * scale
        for i in range(step):
            c = base + i
            rows = pl.ds(c * shards, shards)
            out_ref[rows, :width] = part[i * shards : (i + 1) * shards, :width] + skip_ref[first_channel + c]
            out_ref[rows, width:] = part[i * shards : (i + 1) * shards, width:]


def signals_from(spec, shards, width, cos, sin, last_ref):
    columns = []
    for real, imag in spec:
        columns.append(
            jnp.concatenate([(real * cos - imag * sin).astype(BF16), (imag * cos + real * sin).astype(BF16)], 0)
        )
    parts = dot(last_ref[...], columns[0] if len(columns) == 1 else jnp.concatenate(columns, 1))
    return parts[:shards] + parts[shards:]


def corr_kernel(x_ref, table_ref, twist_ref, spectra_ref, corr_ref, mir_ref, xs, mir_s, lhs, spec):
    shards, both, width = x_ref.shape
    channels = both // 2
    table = table_views(table_ref, shards, width)
    first_ref, last_ref = table["first_twice"], table["last_twice"]
    scale = 1.0 / math.sqrt(shards * width)
    xs[...] = x_ref[...].reshape(shards * both, width).astype(F32)
    cos, sin = twist_ref[0], twist_ref[1]
    step = 8

    @pl.loop(0, channels, step=step)
    def _(base):
        for i in range(step):
            c = base + i
            product = xs[pl.ds(c, shards, stride=both), :].astype(BF16)
            gate = xs[pl.ds(channels + c, shards, stride=both), :].astype(BF16)
            rhs = jnp.concatenate([product, gate], 1)
            part = dot(first_ref[...], jnp.concatenate([rhs, rhs], 0))
            for j in range(2):
                real = part[:shards, j * width : (j + 1) * width]
                imag = part[shards:, j * width : (j + 1) * width]
                rows = pl.ds((2 * i + j) * shards, shards)
                lhs[rows, :width] = (real * cos + imag * sin).astype(BF16)
                lhs[rows, width:] = (imag * cos - real * sin).astype(BF16)
        both_spec = dot(lhs[...], table["forth"][...])
        spectra_ref[pl.ds(2 * base * shards, 2 * step * shards), :] = both_spec
        for i in range(step):
            pr = both_spec[2 * i * shards : (2 * i + 1) * shards, :width]
            pi = both_spec[2 * i * shards : (2 * i + 1) * shards, width:]
            gr = both_spec[(2 * i + 1) * shards : (2 * i + 2) * shards, :width]
            gi = both_spec[(2 * i + 1) * shards : (2 * i + 2) * shards, width:]
            rows = pl.ds((base + i) * shards, shards)
            corr_ref[rows, :width] = (pr * gr + pi * gi).astype(BF16)
            corr_ref[rows, width:] = (pr * gi - pi * gr).astype(BF16)
        spec[...] = dot(corr_ref[pl.ds(base * shards, step * shards), :], table["conj"][...])
        for i in range(0, step, 2):
            pairs = [
                (spec[j * shards : (j + 1) * shards, :width], spec[j * shards : (j + 1) * shards, width:])
                for j in (i, i + 1)
            ]
            part = signals_from(pairs, shards, width, cos, sin, last_ref) * scale
            for j in range(2):
                c = base + i + j
                mir_s[pl.ds(channels - 1 - c, shards, stride=channels), :] = part[:, j * width : (j + 1) * width]

    for n1 in range(shards):
        mir_ref[:, n1 * width : (n1 + 1) * width] = mir_s[n1 * channels : (n1 + 1) * channels, :].astype(BF16)


def mix_kernel(spectra_ref, spec_ref, table_ref, twist_ref, out_ref, ys, lhs, spec, first_s, extra_s):
    shards, rows_sent, width = out_ref.shape
    channels = spec_ref.shape[0] // shards
    both = 2 * channels
    table = table_views(table_ref, shards, width)
    last_ref = table["last_twice"]
    cos, sin = twist_ref[0], twist_ref[1]
    step = 8
    lane_channel = lax.broadcasted_iota(jnp.int32, (shards, width), 1) % channels
    first_s[...] = jnp.zeros_like(first_s)

    @pl.loop(0, channels, step=step)
    def _(base):
        for i in range(step):
            c = base + i
            kr = spec_ref[pl.ds(c * shards, shards), :width]
            ki = spec_ref[pl.ds(c * shards, shards), width:]
            pr = spectra_ref[pl.ds(2 * c * shards, shards), :width]
            pi = spectra_ref[pl.ds(2 * c * shards, shards), width:]
            gr = spectra_ref[pl.ds((2 * c + 1) * shards, shards), :width]
            gi = spectra_ref[pl.ds((2 * c + 1) * shards, shards), width:]
            rows = pl.ds(2 * i * shards, shards)
            lhs[rows, :width] = (kr * pr - ki * pi).astype(BF16)
            lhs[rows, width:] = (kr * pi + ki * pr).astype(BF16)
            rows = pl.ds((2 * i + 1) * shards, shards)
            lhs[rows, :width] = (kr * gr + ki * gi).astype(BF16)
            lhs[rows, width:] = (kr * gi - ki * gr).astype(BF16)
        spec[...] = dot(lhs[...], table["back"][...])
        firsts = [jnp.zeros((shards, width), F32)] * 4
        for i in range(step):
            c = base + i
            pairs = []
            for j in range(2):
                rows = slice((2 * i + j) * shards, (2 * i + j + 1) * shards)
                pairs.append((spec[rows, :width], spec[rows, width:]))
            part = signals_from(pairs, shards, width, cos, sin, last_ref)
            for j in range(2):
                ys[pl.ds(j * channels + c, shards, stride=both), :] = part[:, j * width : (j + 1) * width]
                for p in range(2):
                    column = jnp.broadcast_to(part[:, j * width + p : j * width + p + 1], (shards, width))
                    firsts[2 * j + p] = jnp.where(lane_channel == c, column, firsts[2 * j + p])
        for k in range(4):
            first_s[k, :shards, :] += firsts[k]

    out_ref[:, :both, :] = ys[...].astype(BF16).reshape(shards, both, width)
    extra_s[...] = jnp.zeros_like(extra_s)
    for k in range(4):
        extra_s[pl.ds(k, shards, stride=8), :] = first_s[k, 1 : shards + 1, :]
    out_ref[:, both:, :] = extra_s[...].astype(BF16).reshape(shards, 8, width)


def post_kernel(r_ref, g_ref, qs_ref, ks_ref, vs_ref, ends_ref, next_ref, taps_ref, mixed_hbm, q_hbm, k_hbm, v_hbm, mixed_ref, q_ref, k_ref, v_ref, ext, around, sems):
    rows, channels = g_ref.shape
    group = (r_ref.shape[1] - 8) // 2
    count = 128 // group
    shape = (count, 8, 128)
    size = channels // sems.shape[0]
    pairs = ((mixed_ref, mixed_hbm), (q_ref, q_hbm), (k_ref, k_hbm), (v_ref, v_hbm))
    copies = []
    mine = lax.broadcasted_iota(jnp.int32, shape, 2) // group == lax.broadcasted_iota(jnp.int32, shape, 0)
    for lane in range(0, channels, 128):
        lanes = pl.ds(lane, 128)
        blocks = pl.ds(lane // group, count)
        mix = r_ref[blocks, :group, :].reshape(128, rows).astype(F32).T
        back = r_ref[blocks, group : 2 * group, :].reshape(128, rows).astype(F32).T
        beyond = jnp.sum(jnp.where(mine, r_ref[blocks, 2 * group :, :].astype(F32), 0.0), 0)
        mixed_ref[:, lanes] = (qs_ref[:, lanes].astype(F32) * mix).astype(BF16)
        near = (g_ref, ks_ref, vs_ref)
        gate, key, value = [ref[:, lanes].astype(F32) for ref in near]
        gate_next = next_ref[0, :, lanes].astype(F32)
        shorts_next = []
        for p in (1, 2):
            around[0:2, :] = ends_ref[p - 1, :, lanes].astype(F32)
            around[2:4, :] = next_ref[p, :, lanes].astype(F32)
            shorts_next.append(
                (
                    taps_ref[p, 0:1, lanes] * around[2:4, :]
                    + taps_ref[p, 1:2, lanes] * around[1:3, :]
                    + taps_ref[p, 2:3, lanes] * around[0:2, :]
                )
                .astype(BF16)
                .astype(F32)
            )
        key_next, value_next = shorts_next
        parts = (gate * mix, back * value, back * key)
        beyonds = (gate_next * beyond[0:2], beyond[2:4] * value_next, beyond[2:4] * key_next)
        for p, ref in enumerate((q_ref, k_ref, v_ref)):
            ext[p, 0:rows, :] = parts[p]
            ext[p, rows : rows + 2, :] = beyonds[p]
            ref[:, lanes] = (
                taps_ref[p, 0:1, lanes] * parts[p]
                + taps_ref[p, 1:2, lanes] * ext[p, 1 : rows + 1, :]
                + taps_ref[p, 2:3, lanes] * ext[p, 2 : rows + 2, :]
            ).astype(BF16)
        if (lane + 128) % size == 0:
            chunk = lane // size
            lanes = pl.ds(chunk * size, size)
            for p, (src, dst) in enumerate(pairs):
                copies.append(pltpu.make_async_copy(src.at[:, lanes], dst.at[:, lanes], sems.at[chunk, p]))
                copies[-1].start()
    for copy in copies:
        copy.wait()


def lags_kernel(corr_ref, far_ref, table_ref, twist_ref, out_ref, own_s, spec):
    channels, length = out_ref.shape
    shards = twist_ref.shape[1]
    width = length // shards
    table = table_views(table_ref, shards, width)
    scale = 1.0 / math.sqrt(length)
    cos, sin = twist_ref[0], twist_ref[1]
    step = 4

    @pl.loop(0, channels, step=step)
    def _(base):
        spec[...] = dot(corr_ref[pl.ds(base * shards, step * shards), :], table["back"][...])
        for i in range(0, step, 2):
            pairs = [
                (spec[j * shards : (j + 1) * shards, :width], spec[j * shards : (j + 1) * shards, width:])
                for j in (i, i + 1)
            ]
            part = signals_from(pairs, shards, width, cos, sin, table["last_twice"]) * scale
            for j in range(2):
                c = base + i + j
                own_s[pl.ds(c, shards, stride=channels), :] = part[:, j * width : (j + 1) * width]

    for n1 in range(shards):
        lanes = slice(n1 * width, (n1 + 1) * width)
        out_ref[:, lanes] = own_s[n1 * channels : (n1 + 1) * channels, :] + far_ref[:, lanes].astype(F32)


def per_device(query_proj, key_proj, value_proj, short_taps, skip_gain, long_filter, out_grad):
    positions, width = query_proj.shape
    channels, length = long_filter.shape
    shards = lax.axis_size("seq")
    table, twist = make_tables(shards, positions)
    shape = jax.ShapeDtypeStruct

    near = [pltpu.with_memory_space_constraint(x, pltpu.HBM) for x in (query_proj, key_proj, value_proj, out_grad)]
    ends, starts = call(
        ends_kernel,
        (shape((3, 2, width), BF16), shape((3, 2, width), BF16)),
        [pltpu.VMEM((6, 16, width), BF16), pltpu.SemaphoreType.DMA((6,))],
        bytes_accessed=200 * width,
        in_specs=[pl.BlockSpec(memory_space=pltpu.HBM)] * 4,
    )(*near)
    previous = passed_along(ends, "seq", 1)
    previous, filter_sent = lax.optimization_barrier((previous, long_filter.astype(BF16)))
    filter_far = to_mirror(filter_sent)
    wide = shape((positions, width), BF16)
    hbm, vmem = pl.BlockSpec(memory_space=pltpu.HBM), pl.BlockSpec(memory_space=pltpu.VMEM)
    query_short, key_short, value_short, send, own_ends = call(
        pre_kernel,
        (wide, wide, wide, shape((shards, 2 * channels, positions), BF16), shape((2, 2, width), BF16)),
        [
            *[pltpu.VMEM((positions, width), BF16)] * 4,
            pltpu.VMEM(short_taps.shape, F32),
            pltpu.VMEM((shards, 2 * channels, positions), BF16),
            pltpu.VMEM((3, positions + 8, 128), F32),
            pltpu.SemaphoreType.DMA((4, 4)),
            pltpu.SemaphoreType.DMA((5,)),
        ],
        flops=30 * positions * width,
        bytes_accessed=18 * positions * width,
        in_specs=[hbm] * 5 + [vmem],
        out_specs=(vmem, vmem, vmem, hbm, vmem),
    )(*near, pltpu.with_memory_space_constraint(short_taps, pltpu.HBM), previous)
    received = lax.all_to_all(send, "seq", split_axis=0, concat_axis=0, tiled=True)

    step = 8
    spectrum = call(
        spectrum_kernel,
        shape((channels * shards, 2 * positions), F32),
        [
            pltpu.VMEM((shards * channels, positions), F32),
            pltpu.VMEM((shards * channels, positions), F32),
            pltpu.VMEM((4 * shards, 4 * positions), BF16),
        ],
        flops=SPEC_FLOPS,
        bytes_accessed=14 * channels * length,
        in_specs=[pl.BlockSpec(memory_space=pltpu.VMEM)] * 2
        + [pl.BlockSpec(memory_space=pltpu.SMEM)]
        + [pl.BlockSpec(memory_space=pltpu.VMEM)] * 2,
    )(long_filter, filter_far, skip_gain, table, twist)

    received, spectrum = lax.optimization_barrier((received, spectrum))
    spectra, corr, lagged_back = call(
        corr_kernel,
        (
            shape((2 * channels * shards, 2 * positions), F32),
            shape((channels * shards, 2 * positions), BF16),
            shape((channels, length), BF16),
        ),
        [
            pltpu.VMEM((shards * 2 * channels, positions), F32),
            pltpu.VMEM((shards * channels, positions), F32),
            pltpu.VMEM((2 * step * shards, 2 * positions), BF16),
            pltpu.VMEM((step * shards, 2 * positions), F32),
        ],
        flops=CORR_FLOPS,
        bytes_accessed=24 * channels * length,
    )(received, table, twist)
    returned = call(
        mix_kernel,
        shape((shards, 2 * channels + 8, positions), BF16),
        [
            pltpu.VMEM((shards * 2 * channels, positions), F32),
            pltpu.VMEM((2 * step * shards, 2 * positions), BF16),
            pltpu.VMEM((2 * step * shards, 2 * positions), F32),
            pltpu.VMEM((4, shards + 8, positions), F32),
            pltpu.VMEM((shards * 8, positions), F32),
        ],
        flops=MIX_FLOPS,
        bytes_accessed=24 * channels * length,
    )(spectra, spectrum, table, twist)
    lagged_back, returned = lax.optimization_barrier((lagged_back, returned))
    lagged_far = to_mirror(lagged_back)
    result = lax.all_to_all(returned, "seq", split_axis=0, concat_axis=0, tiled=True)

    filter_grad = call(
        lags_kernel,
        shape((channels, length), F32),
        [
            pltpu.VMEM((shards * channels, positions), F32),
            pltpu.VMEM((4 * shards, 2 * positions), F32),
        ],
        flops=ADD_FLOPS,
        bytes_accessed=10 * channels * length,
    )(corr, lagged_far, table, twist)
    starts, filter_grad = lax.optimization_barrier((starts, filter_grad))
    following = passed_along(starts, "seq", -1)
    mixed_out, query_grad, key_grad, value_grad = call(
        post_kernel,
        (wide, wide, wide, wide),
        [
            *[pltpu.VMEM((positions, width), BF16)] * 4,
            pltpu.VMEM((3, positions + 8, 128), F32),
            pltpu.VMEM((8, 128), F32),
            pltpu.SemaphoreType.DMA((4, 4)),
        ],
        flops=30 * positions * width,
        bytes_accessed=20 * positions * width,
        out_specs=(hbm, hbm, hbm, hbm),
    )(result, out_grad, query_short, key_short, value_short, own_ends, following, short_taps)
    return (mixed_out, query_grad, key_grad, value_grad, filter_grad)


def solution(mesh):
    in_specs = (
        P("seq", "chan"),
        P("seq", "chan"),
        P("seq", "chan"),
        P(None, None, "chan"),
        P("chan"),
        P(("chan", "seq"), None),
        P("seq", "chan"),
    )
    out_specs = (
        P("seq", "chan"),
        P("seq", "chan"),
        P("seq", "chan"),
        P("seq", "chan"),
        P(("chan", "seq"), None),
    )
    return jax.shard_map(
        per_device, mesh=mesh, in_specs=in_specs, out_specs=out_specs, check_vma=False
    )
```

```python
import math

import jax
import jax.numpy as jnp
import ml_dtypes
import numpy as np
from jax import lax
from jax.experimental import pallas as pl
from jax.experimental.pallas import tpu as pltpu
from jax.sharding import PartitionSpec as P

F32 = jnp.float32
BF16 = jnp.bfloat16

SPEC_FLOPS = 1 << 34
CORR_FLOPS = 1 << 29
MIX_FLOPS = 1 << 29
STAGE_FLOPS = 1 << 20
ADD_FLOPS = 1 << 34


def passed_along(array, axis, by):
    length = lax.axis_size(axis)
    pairs = [(i, i + by) for i in range(length) if 0 <= i + by < length]
    return lax.ppermute(array, axis, pairs)


def to_mirror(array):
    count = lax.axis_size("seq") * lax.axis_size("chan")
    return lax.ppermute(array, ("seq", "chan"), [(i, count - 1 - i) for i in range(count)])


def split_bf16(matrix):
    high = matrix.astype(ml_dtypes.bfloat16)
    low = (matrix - high.astype(np.float64)).astype(ml_dtypes.bfloat16)
    return high, low


def make_tables(shards, width):
    n1 = np.arange(shards)[:, None]
    k1 = np.arange(shards)[None, :] + 0.5
    n2 = np.arange(width)
    outer = 2.0 * np.pi * k1.T * n1.T / (2 * shards)
    first = np.concatenate([np.cos(outer), -np.sin(outer)], 0)
    high, low = split_bf16(first)
    first_thrice = np.concatenate([high, low, high], 1)
    last = first.T / (shards * width)
    high, low = split_bf16(last)
    last_twice = np.pad(np.concatenate([high, low], 0), ((0, 0), (0, 2 * width - 2 * shards)))
    twist = 2.0 * np.pi * k1.T * n2[None, :] / (2 * shards * width)
    twist = np.stack([np.cos(twist), np.sin(twist)]).astype(np.float32)
    inner = 2.0 * np.pi * (n2[:, None] * n2[None, :] % width) / width
    cos, sin = np.cos(inner), np.sin(inner)
    forth = np.block([[cos, -sin], [sin, cos]])
    conj = np.block([[cos, sin], [sin, -cos]])
    back = np.block([[cos, sin], [-sin, cos]])
    square = np.concatenate([forth, conj, back], 0).astype(ml_dtypes.bfloat16)
    first_thrice = np.pad(first_thrice, ((0, 0), (0, 2 * width - 3 * shards)))
    return np.concatenate([square, first_thrice, last_twice], 0), twist


def table_views(table_ref, shards, width):
    at = 6 * width
    return dict(
        forth=table_ref.at[0 : 2 * width],
        kernel_forth=table_ref.at[0 : 4 * width],
        conj=table_ref.at[2 * width : 4 * width],
        back=table_ref.at[4 * width : at],
        first_twice=table_ref.at[at : at + 2 * shards, : 2 * shards],
        first_thrice=table_ref.at[at : at + 2 * shards, : 3 * shards],
        last_twice=table_ref.at[at + 2 * shards : at + 4 * shards, : 2 * shards],
    )


def dot(left, right):
    return jnp.dot(left, right, preferred_element_type=F32)


def call(kernel, out_shape, scratch=(), flops=0, bytes_accessed=0, limit=44, **more):
    return pl.pallas_call(
        kernel,
        out_shape=out_shape,
        scratch_shapes=list(scratch),
        compiler_params=pltpu.CompilerParams(vmem_limit_bytes=limit << 20),
        cost_estimate=pl.CostEstimate(
            flops=flops, bytes_accessed=bytes_accessed, transcendentals=0
        ),
        **more,
    )


def ends_kernel(q_hbm, k_hbm, v_hbm, g_hbm, last_ref, first_ref, held, sems):
    rows = q_hbm.shape[0]
    sources = [ref.at[rows - 16 :] for ref in (q_hbm, k_hbm, v_hbm)] + [ref.at[:16] for ref in (g_hbm, k_hbm, v_hbm)]
    copies = [pltpu.make_async_copy(src, held.at[p], sems.at[p]) for p, src in enumerate(sources)]
    for copy in copies:
        copy.start()
    for p, copy in enumerate(copies):
        copy.wait()
        if p < 3:
            last_ref[p] = held[p].astype(F32)[14:16].astype(BF16)
        else:
            first_ref[p - 3] = held[p].astype(F32)[0:2].astype(BF16)


def stage_kernel(q_hbm, k_hbm, v_hbm, g_hbm, taps_hbm, own_hbm, q_ref, k_ref, v_ref, g_ref, taps_ref, sent_ref, own_ref, sems):
    pairs = ((own_hbm, own_ref), (q_hbm, q_ref), (k_hbm, k_ref), (v_hbm, v_ref), (g_hbm, g_ref), (taps_hbm, taps_ref))
    copies = [pltpu.make_async_copy(src, dst, sems.at[p]) for p, (src, dst) in enumerate(pairs)]
    for copy in copies:
        copy.start()
    copies[0].wait()
    sent_ref[...] = own_ref[...].astype(BF16)
    for copy in copies[1:]:
        copy.wait()


def pre_kernel(q_ref, k_ref, v_ref, g_ref, taps_ref, halo_ref, qs_ref, ks_ref, vs_ref, send_hbm, ends_ref, send_ref, ext, out_sems):
    rows, channels = q_ref.shape
    group = send_ref.shape[1] // 2
    chunks = out_sems.shape[0]
    size = channels // chunks
    sends = []
    for chunk in range(chunks):
        for lane in range(chunk * size, (chunk + 1) * size, 128):
            lanes = pl.ds(lane, 128)
            shorts = []
            for p, ref in enumerate((q_ref, k_ref, v_ref)):
                ext[p, 6:8, :] = halo_ref[p, :, lanes].astype(F32)
                ext[p, 8 : rows + 8, :] = ref[:, lanes].astype(F32)
                shorts.append(
                    (
                        taps_ref[p, 0:1, lanes] * ext[p, 8 : rows + 8, :]
                        + taps_ref[p, 1:2, lanes] * ext[p, 7 : rows + 7, :]
                        + taps_ref[p, 2:3, lanes] * ext[p, 6 : rows + 6, :]
                    ).astype(BF16)
                )
            qs, ks, vs = shorts
            qs_ref[:, lanes] = qs
            ks_ref[:, lanes] = ks
            vs_ref[:, lanes] = vs
            product = ks.astype(F32) * vs.astype(F32)
            gate = g_ref[:, lanes].astype(F32) * qs.astype(F32)
            for p in (1, 2):
                ends_ref[p - 1, :, lanes] = ext[p, rows + 6 : rows + 8, :].astype(BF16)
            blocks = pl.ds(lane // group, 128 // group)
            send_ref[blocks, 0:group, :] = product.T.astype(BF16).reshape(128 // group, group, rows)
            send_ref[blocks, group:, :] = gate.T.astype(BF16).reshape(128 // group, group, rows)
        blocks = pl.ds(chunk * size // group, size // group)
        sends.append(pltpu.make_async_copy(send_ref.at[blocks], send_hbm.at[blocks], out_sems.at[chunk]))
        sends[-1].start()
    for copy in sends:
        copy.wait()


def spectrum_kernel(own_ref, mir_ref, skip_ref, table_ref, twist_ref, out_ref, own_s, mir_s, lhs):
    channels, length = own_ref.shape
    shards = twist_ref.shape[1]
    width = length // shards
    table = table_views(table_ref, shards, width)
    first_ref, forth_ref = table["first_thrice"], table["kernel_forth"]
    scale = 1.0 / math.sqrt(length)
    first_channel = lax.axis_index("seq") * channels
    for n1 in range(shards):
        own_s[n1 * channels : (n1 + 1) * channels, :] = own_ref[:, n1 * width : (n1 + 1) * width]
        mir_s[n1 * channels : (n1 + 1) * channels, :] = mir_ref[:, n1 * width : (n1 + 1) * width].astype(F32)
    cos, sin = twist_ref[0], twist_ref[1]
    step = 4

    @pl.loop(0, channels, step=step)
    def _(base):
        for i in range(step):
            c = base + i
            own = own_s[pl.ds(c, shards, stride=channels), :]
            mir = mir_s[pl.ds(channels - 1 - c, shards, stride=channels), :].astype(BF16)
            high = own.astype(BF16)
            low = (own - high.astype(F32)).astype(BF16)
            part = dot(first_ref[...], jnp.concatenate([high, high, low], 0))
            real, imag = part[:shards], part[shards:]
            rows = pl.ds(i * shards, shards)
            lhs[rows, 0:width] = (real * cos + imag * sin).astype(BF16)
            lhs[rows, width : 2 * width] = (imag * cos - real * sin).astype(BF16)
            part = dot(table["first_twice"][...], jnp.concatenate([mir, mir], 0))
            real, imag = part[:shards], part[shards:]
            lhs[rows, 2 * width : 3 * width] = (real * cos + imag * sin).astype(BF16)
            lhs[rows, 3 * width :] = (imag * cos - real * sin).astype(BF16)
        part = dot(lhs[...], forth_ref[...]) * scale
        for i in range(step):
            c = base + i
            rows = pl.ds(c * shards, shards)
            out_ref[rows, :width] = part[i * shards : (i + 1) * shards, :width] + skip_ref[first_channel + c]
            out_ref[rows, width:] = part[i * shards : (i + 1) * shards, width:]


def signals_from(spec, shards, width, cos, sin, last_ref):
    columns = []
    for real, imag in spec:
        columns.append(
            jnp.concatenate([(real * cos - imag * sin).astype(BF16), (imag * cos + real * sin).astype(BF16)], 0)
        )
    parts = dot(last_ref[...], columns[0] if len(columns) == 1 else jnp.concatenate(columns, 1))
    return parts[:shards] + parts[shards:]


def corr_kernel(x_ref, table_ref, twist_ref, spectra_ref, corr_ref, mir_ref, xs, mir_s, lhs, spec):
    shards, both, width = x_ref.shape
    channels = both // 2
    table = table_views(table_ref, shards, width)
    first_ref, last_ref = table["first_twice"], table["last_twice"]
    scale = 1.0 / math.sqrt(shards * width)
    xs[...] = x_ref[...].reshape(shards * both, width).astype(F32)
    cos, sin = twist_ref[0], twist_ref[1]
    step = 16

    @pl.loop(0, channels, step=step)
    def _(base):
        for i in range(step):
            c = base + i
            product = xs[pl.ds(c, shards, stride=both), :].astype(BF16)
            gate = xs[pl.ds(channels + c, shards, stride=both), :].astype(BF16)
            rhs = jnp.concatenate([product, gate], 1)
            part = dot(first_ref[...], jnp.concatenate([rhs, rhs], 0))
            for j in range(2):
                real = part[:shards, j * width : (j + 1) * width]
                imag = part[shards:, j * width : (j + 1) * width]
                rows = pl.ds((2 * i + j) * shards, shards)
                lhs[rows, :width] = (real * cos + imag * sin).astype(BF16)
                lhs[rows, width:] = (imag * cos - real * sin).astype(BF16)
        both_spec = dot(lhs[...], table["forth"][...])
        spectra_ref[pl.ds(2 * base * shards, 2 * step * shards), :] = both_spec
        for i in range(step):
            pr = both_spec[2 * i * shards : (2 * i + 1) * shards, :width]
            pi = both_spec[2 * i * shards : (2 * i + 1) * shards, width:]
            gr = both_spec[(2 * i + 1) * shards : (2 * i + 2) * shards, :width]
            gi = both_spec[(2 * i + 1) * shards : (2 * i + 2) * shards, width:]
            rows = pl.ds((base + i) * shards, shards)
            corr_ref[rows, :width] = (pr * gr + pi * gi).astype(BF16)
            corr_ref[rows, width:] = (pr * gi - pi * gr).astype(BF16)
        spec[...] = dot(corr_ref[pl.ds(base * shards, step * shards), :], table["conj"][...])
        for i in range(0, step, 2):
            pairs = [
                (spec[j * shards : (j + 1) * shards, :width], spec[j * shards : (j + 1) * shards, width:])
                for j in (i, i + 1)
            ]
            part = signals_from(pairs, shards, width, cos, sin, last_ref) * scale
            for j in range(2):
                c = base + i + j
                mir_s[pl.ds(channels - 1 - c, shards, stride=channels), :] = part[:, j * width : (j + 1) * width]

    for n1 in range(shards):
        mir_ref[:, n1 * width : (n1 + 1) * width] = mir_s[n1 * channels : (n1 + 1) * channels, :].astype(BF16)


def mix_kernel(spectra_ref, spec_ref, table_ref, twist_ref, out_ref, ys, lhs, spec, first_s, extra_s):
    shards, rows_sent, width = out_ref.shape
    channels = spec_ref.shape[0] // shards
    both = 2 * channels
    table = table_views(table_ref, shards, width)
    last_ref = table["last_twice"]
    cos, sin = twist_ref[0], twist_ref[1]
    step = 16
    lane_channel = lax.broadcasted_iota(jnp.int32, (shards, width), 1) % channels
    first_s[...] = jnp.zeros_like(first_s)

    @pl.loop(0, channels, step=step)
    def _(base):
        for i in range(step):
            c = base + i
            kr = spec_ref[pl.ds(c * shards, shards), :width]
            ki = spec_ref[pl.ds(c * shards, shards), width:]
            pr = spectra_ref[pl.ds(2 * c * shards, shards), :width]
            pi = spectra_ref[pl.ds(2 * c * shards, shards), width:]
            gr = spectra_ref[pl.ds((2 * c + 1) * shards, shards), :width]
            gi = spectra_ref[pl.ds((2 * c + 1) * shards, shards), width:]
            rows = pl.ds(2 * i * shards, shards)
            lhs[rows, :width] = (kr * pr - ki * pi).astype(BF16)
            lhs[rows, width:] = (kr * pi + ki * pr).astype(BF16)
            rows = pl.ds((2 * i + 1) * shards, shards)
            lhs[rows, :width] = (kr * gr + ki * gi).astype(BF16)
            lhs[rows, width:] = (kr * gi - ki * gr).astype(BF16)
        spec[...] = dot(lhs[...], table["back"][...])
        firsts = [jnp.zeros((shards, width), F32)] * 4
        for i in range(step):
            c = base + i
            pairs = []
            for j in range(2):
                rows = slice((2 * i + j) * shards, (2 * i + j + 1) * shards)
                pairs.append((spec[rows, :width], spec[rows, width:]))
            part = signals_from(pairs, shards, width, cos, sin, last_ref)
            for j in range(2):
                ys[pl.ds(j * channels + c, shards, stride=both), :] = part[:, j * width : (j + 1) * width]
                for p in range(2):
                    column = jnp.broadcast_to(part[:, j * width + p : j * width + p + 1], (shards, width))
                    firsts[2 * j + p] = jnp.where(lane_channel == c, column, firsts[2 * j + p])
        for k in range(4):
            first_s[k, :shards, :] += firsts[k]

    out_ref[:, :both, :] = ys[...].astype(BF16).reshape(shards, both, width)
    extra_s[...] = jnp.zeros_like(extra_s)
    for k in range(4):
        extra_s[pl.ds(k, shards, stride=8), :] = first_s[k, 1 : shards + 1, :]
    out_ref[:, both:, :] = extra_s[...].astype(BF16).reshape(shards, 8, width)


def post_kernel(r_ref, g_ref, qs_ref, ks_ref, vs_ref, ends_ref, next_ref, taps_ref, mixed_hbm, q_hbm, k_hbm, v_hbm, mixed_ref, q_ref, k_ref, v_ref, ext, around, sems):
    rows, channels = g_ref.shape
    group = (r_ref.shape[1] - 8) // 2
    count = 128 // group
    shape = (count, 8, 128)
    size = channels // sems.shape[0]
    pairs = ((mixed_ref, mixed_hbm), (q_ref, q_hbm), (k_ref, k_hbm), (v_ref, v_hbm))
    copies = []
    mine = lax.broadcasted_iota(jnp.int32, shape, 2) // group == lax.broadcasted_iota(jnp.int32, shape, 0)
    for lane in range(0, channels, 128):
        lanes = pl.ds(lane, 128)
        blocks = pl.ds(lane // group, count)
        mix = r_ref[blocks, :group, :].reshape(128, rows).astype(F32).T
        back = r_ref[blocks, group : 2 * group, :].reshape(128, rows).astype(F32).T
        beyond = jnp.sum(jnp.where(mine, r_ref[blocks, 2 * group :, :].astype(F32), 0.0), 0)
        mixed_ref[:, lanes] = (qs_ref[:, lanes].astype(F32) * mix).astype(BF16)
        near = (g_ref, ks_ref, vs_ref)
        gate, key, value = [ref[:, lanes].astype(F32) for ref in near]
        gate_next = next_ref[0, :, lanes].astype(F32)
        shorts_next = []
        for p in (1, 2):
            around[0:2, :] = ends_ref[p - 1, :, lanes].astype(F32)
            around[2:4, :] = next_ref[p, :, lanes].astype(F32)
            shorts_next.append(
                (
                    taps_ref[p, 0:1, lanes] * around[2:4, :]
                    + taps_ref[p, 1:2, lanes] * around[1:3, :]
                    + taps_ref[p, 2:3, lanes] * around[0:2, :]
                )
                .astype(BF16)
                .astype(F32)
            )
        key_next, value_next = shorts_next
        parts = (gate * mix, back * value, back * key)
        beyonds = (gate_next * beyond[0:2], beyond[2:4] * value_next, beyond[2:4] * key_next)
        for p, ref in enumerate((q_ref, k_ref, v_ref)):
            ext[p, 0:rows, :] = parts[p]
            ext[p, rows : rows + 2, :] = beyonds[p]
            ref[:, lanes] = (
                taps_ref[p, 0:1, lanes] * parts[p]
                + taps_ref[p, 1:2, lanes] * ext[p, 1 : rows + 1, :]
                + taps_ref[p, 2:3, lanes] * ext[p, 2 : rows + 2, :]
            ).astype(BF16)
        if (lane + 128) % size == 0:
            chunk = lane // size
            lanes = pl.ds(chunk * size, size)
            for p, (src, dst) in enumerate(pairs):
                copies.append(pltpu.make_async_copy(src.at[:, lanes], dst.at[:, lanes], sems.at[chunk, p]))
                copies[-1].start()
    for copy in copies:
        copy.wait()


def lags_kernel(corr_ref, far_ref, table_ref, twist_ref, out_ref, own_s, spec):
    channels, length = out_ref.shape
    shards = twist_ref.shape[1]
    width = length // shards
    table = table_views(table_ref, shards, width)
    scale = 1.0 / math.sqrt(length)
    cos, sin = twist_ref[0], twist_ref[1]
    step = 4

    @pl.loop(0, channels, step=step)
    def _(base):
        spec[...] = dot(corr_ref[pl.ds(base * shards, step * shards), :], table["back"][...])
        for i in range(0, step, 2):
            pairs = [
                (spec[j * shards : (j + 1) * shards, :width], spec[j * shards : (j + 1) * shards, width:])
                for j in (i, i + 1)
            ]
            part = signals_from(pairs, shards, width, cos, sin, table["last_twice"]) * scale
            for j in range(2):
                c = base + i + j
                own_s[pl.ds(c, shards, stride=channels), :] = part[:, j * width : (j + 1) * width]

    for n1 in range(shards):
        lanes = slice(n1 * width, (n1 + 1) * width)
        out_ref[:, lanes] = own_s[n1 * channels : (n1 + 1) * channels, :] + far_ref[:, lanes].astype(F32)


def per_device(query_proj, key_proj, value_proj, short_taps, skip_gain, long_filter, out_grad):
    positions, width = query_proj.shape
    channels, length = long_filter.shape
    shards = lax.axis_size("seq")
    table, twist = make_tables(shards, positions)
    shape = jax.ShapeDtypeStruct

    near = [pltpu.with_memory_space_constraint(x, pltpu.HBM) for x in (query_proj, key_proj, value_proj, out_grad)]
    ends, starts = call(
        ends_kernel,
        (shape((3, 2, width), BF16), shape((3, 2, width), BF16)),
        [pltpu.VMEM((6, 16, width), BF16), pltpu.SemaphoreType.DMA((6,))],
        bytes_accessed=200 * width,
        in_specs=[pl.BlockSpec(memory_space=pltpu.HBM)] * 4,
    )(*near)
    previous = passed_along(ends, "seq", 1)
    wide = shape((positions, width), BF16)
    hbm, vmem = pl.BlockSpec(memory_space=pltpu.HBM), pl.BlockSpec(memory_space=pltpu.VMEM)
    far = [pltpu.with_memory_space_constraint(x, pltpu.HBM) for x in (out_grad, short_taps, long_filter)]
    *staged, filter_sent = call(
        stage_kernel,
        (wide, wide, wide, wide, shape(short_taps.shape, F32), shape((channels, length), BF16)),
        [pltpu.VMEM((channels, length), F32), pltpu.SemaphoreType.DMA((6,))],
        flops=STAGE_FLOPS,
        bytes_accessed=16 * positions * width,
        in_specs=[hbm] * 6,
    )(*near[:3], *far)
    previous, filter_sent = lax.optimization_barrier((previous, filter_sent))
    filter_far = to_mirror(filter_sent)
    query_short, key_short, value_short, send, own_ends = call(
        pre_kernel,
        (wide, wide, wide, shape((shards, 2 * channels, positions), BF16), shape((2, 2, width), BF16)),
        [
            pltpu.VMEM((shards, 2 * channels, positions), BF16),
            pltpu.VMEM((3, positions + 8, 128), F32),
            pltpu.SemaphoreType.DMA((4,)),
        ],
        flops=30 * positions * width,
        bytes_accessed=18 * positions * width,
        out_specs=(vmem, vmem, vmem, hbm, vmem),
    )(*staged, previous)
    received = lax.all_to_all(send, "seq", split_axis=0, concat_axis=0, tiled=True)

    step = 16
    spectrum = call(
        spectrum_kernel,
        shape((channels * shards, 2 * positions), F32),
        [
            pltpu.VMEM((shards * channels, positions), F32),
            pltpu.VMEM((shards * channels, positions), F32),
            pltpu.VMEM((4 * shards, 4 * positions), BF16),
        ],
        flops=SPEC_FLOPS,
        bytes_accessed=14 * channels * length,
        in_specs=[pl.BlockSpec(memory_space=pltpu.VMEM)] * 2
        + [pl.BlockSpec(memory_space=pltpu.SMEM)]
        + [pl.BlockSpec(memory_space=pltpu.VMEM)] * 2,
    )(long_filter, filter_far, skip_gain, table, twist)

    received, spectrum = lax.optimization_barrier((received, spectrum))
    spectra, corr, lagged_back = call(
        corr_kernel,
        (
            shape((2 * channels * shards, 2 * positions), F32),
            shape((channels * shards, 2 * positions), BF16),
            shape((channels, length), BF16),
        ),
        [
            pltpu.VMEM((shards * 2 * channels, positions), F32),
            pltpu.VMEM((shards * channels, positions), F32),
            pltpu.VMEM((2 * step * shards, 2 * positions), BF16),
            pltpu.VMEM((step * shards, 2 * positions), F32),
        ],
        flops=CORR_FLOPS,
        bytes_accessed=24 * channels * length,
    )(received, table, twist)
    returned = call(
        mix_kernel,
        shape((shards, 2 * channels + 8, positions), BF16),
        [
            pltpu.VMEM((shards * 2 * channels, positions), F32),
            pltpu.VMEM((2 * step * shards, 2 * positions), BF16),
            pltpu.VMEM((2 * step * shards, 2 * positions), F32),
            pltpu.VMEM((4, shards + 8, positions), F32),
            pltpu.VMEM((shards * 8, positions), F32),
        ],
        flops=MIX_FLOPS,
        bytes_accessed=24 * channels * length,
    )(spectra, spectrum, table, twist)
    lagged_far = to_mirror(lagged_back)
    result = lax.all_to_all(returned, "seq", split_axis=0, concat_axis=0, tiled=True)

    filter_grad = call(
        lags_kernel,
        shape((channels, length), F32),
        [
            pltpu.VMEM((shards * channels, positions), F32),
            pltpu.VMEM((4 * shards, 2 * positions), F32),
        ],
        flops=ADD_FLOPS,
        bytes_accessed=10 * channels * length,
    )(corr, lagged_far, table, twist)
    starts, filter_grad = lax.optimization_barrier((starts, filter_grad))
    following = passed_along(starts, "seq", -1)
    mixed_out, query_grad, key_grad, value_grad = call(
        post_kernel,
        (wide, wide, wide, wide),
        [
            *[pltpu.VMEM((positions, width), BF16)] * 4,
            pltpu.VMEM((3, positions + 8, 128), F32),
            pltpu.VMEM((8, 128), F32),
            pltpu.SemaphoreType.DMA((4, 4)),
        ],
        flops=30 * positions * width,
        bytes_accessed=20 * positions * width,
        out_specs=(hbm, hbm, hbm, hbm),
    )(result, out_grad, query_short, key_short, value_short, own_ends, following, short_taps)
    return (mixed_out, query_grad, key_grad, value_grad, filter_grad)


def solution(mesh):
    in_specs = (
        P("seq", "chan"),
        P("seq", "chan"),
        P("seq", "chan"),
        P(None, None, "chan"),
        P("chan"),
        P(("chan", "seq"), None),
        P("seq", "chan"),
    )
    out_specs = (
        P("seq", "chan"),
        P("seq", "chan"),
        P("seq", "chan"),
        P("seq", "chan"),
        P(("chan", "seq"), None),
    )
    return jax.shard_map(
        per_device, mesh=mesh, in_specs=in_specs, out_specs=out_specs, check_vma=False
    )
```

```python
import math

import jax
import jax.numpy as jnp
import ml_dtypes
import numpy as np
from jax import lax
from jax.experimental import pallas as pl
from jax.experimental.pallas import tpu as pltpu
from jax.sharding import PartitionSpec as P

F32 = jnp.float32
BF16 = jnp.bfloat16

SPEC_FLOPS = 1 << 34
CORR_FLOPS = 1 << 29
MIX_FLOPS = 1 << 29
STAGE_FLOPS = 1 << 20
ADD_FLOPS = 1 << 34


def passed_along(array, axis, by):
    length = lax.axis_size(axis)
    pairs = [(i, i + by) for i in range(length) if 0 <= i + by < length]
    return lax.ppermute(array, axis, pairs)


def to_mirror(array):
    count = lax.axis_size("seq") * lax.axis_size("chan")
    return lax.ppermute(array, ("seq", "chan"), [(i, count - 1 - i) for i in range(count)])


def split_bf16(matrix):
    high = matrix.astype(ml_dtypes.bfloat16)
    low = (matrix - high.astype(np.float64)).astype(ml_dtypes.bfloat16)
    return high, low


def make_tables(shards, width):
    n1 = np.arange(shards)[:, None]
    k1 = np.arange(shards)[None, :] + 0.5
    n2 = np.arange(width)
    outer = 2.0 * np.pi * k1.T * n1.T / (2 * shards)
    first = np.concatenate([np.cos(outer), -np.sin(outer)], 0)
    high, low = split_bf16(first)
    first_thrice = np.concatenate([high, low, high], 1)
    last = first.T / (shards * width)
    high, low = split_bf16(last)
    last_twice = np.pad(np.concatenate([high, low], 0), ((0, 0), (0, 2 * width - 2 * shards)))
    twist = 2.0 * np.pi * k1.T * n2[None, :] / (2 * shards * width)
    twist = np.stack([np.cos(twist), np.sin(twist)]).astype(np.float32)
    inner = 2.0 * np.pi * (n2[:, None] * n2[None, :] % width) / width
    cos, sin = np.cos(inner), np.sin(inner)
    forth = np.block([[cos, -sin], [sin, cos]])
    conj = np.block([[cos, sin], [sin, -cos]])
    back = np.block([[cos, sin], [-sin, cos]])
    square = np.concatenate([forth, conj, back], 0).astype(ml_dtypes.bfloat16)
    first_thrice = np.pad(first_thrice, ((0, 0), (0, 2 * width - 3 * shards)))
    return np.concatenate([square, first_thrice, last_twice], 0), twist


def table_views(table_ref, shards, width):
    at = 6 * width
    return dict(
        forth=table_ref.at[0 : 2 * width],
        kernel_forth=table_ref.at[0 : 4 * width],
        conj=table_ref.at[2 * width : 4 * width],
        back=table_ref.at[4 * width : at],
        first_twice=table_ref.at[at : at + 2 * shards, : 2 * shards],
        first_thrice=table_ref.at[at : at + 2 * shards, : 3 * shards],
        last_twice=table_ref.at[at + 2 * shards : at + 4 * shards, : 2 * shards],
    )


def dot(left, right):
    return jnp.dot(left, right, preferred_element_type=F32)


def call(kernel, out_shape, scratch=(), flops=0, bytes_accessed=0, limit=44, **more):
    return pl.pallas_call(
        kernel,
        out_shape=out_shape,
        scratch_shapes=list(scratch),
        compiler_params=pltpu.CompilerParams(vmem_limit_bytes=limit << 20),
        cost_estimate=pl.CostEstimate(
            flops=flops, bytes_accessed=bytes_accessed, transcendentals=0
        ),
        **more,
    )


def ends_kernel(q_hbm, k_hbm, v_hbm, g_hbm, last_ref, first_ref, held, sems):
    rows = q_hbm.shape[0]
    sources = [ref.at[rows - 16 :] for ref in (q_hbm, k_hbm, v_hbm)] + [ref.at[:16] for ref in (g_hbm, k_hbm, v_hbm)]
    copies = [pltpu.make_async_copy(src, held.at[p], sems.at[p]) for p, src in enumerate(sources)]
    for copy in copies:
        copy.start()
    for p, copy in enumerate(copies):
        copy.wait()
        if p < 3:
            last_ref[p] = held[p].astype(F32)[14:16].astype(BF16)
        else:
            first_ref[p - 3] = held[p].astype(F32)[0:2].astype(BF16)


def stage_kernel(q_hbm, k_hbm, v_hbm, g_hbm, taps_hbm, own_hbm, q_ref, k_ref, v_ref, g_ref, taps_ref, sent_ref, own_ref, sems):
    pairs = ((own_hbm, own_ref), (q_hbm, q_ref), (k_hbm, k_ref), (v_hbm, v_ref), (g_hbm, g_ref), (taps_hbm, taps_ref))
    copies = [pltpu.make_async_copy(src, dst, sems.at[p]) for p, (src, dst) in enumerate(pairs)]
    for copy in copies:
        copy.start()
    copies[0].wait()
    sent_ref[...] = own_ref[...].astype(BF16)
    for copy in copies[1:]:
        copy.wait()


def pre_kernel(q_ref, k_ref, v_ref, g_ref, taps_ref, halo_ref, qs_ref, ks_ref, vs_ref, send_hbm, ends_ref, send_ref, ext, out_sems):
    rows, channels = q_ref.shape
    group = send_ref.shape[1] // 2
    chunks = out_sems.shape[0]
    size = channels // chunks
    sends = []
    for chunk in range(chunks):
        for lane in range(chunk * size, (chunk + 1) * size, 128):
            lanes = pl.ds(lane, 128)
            shorts = []
            for p, ref in enumerate((q_ref, k_ref, v_ref)):
                ext[p, 6:8, :] = halo_ref[p, :, lanes].astype(F32)
                ext[p, 8 : rows + 8, :] = ref[:, lanes].astype(F32)
                shorts.append(
                    (
                        taps_ref[p, 0:1, lanes] * ext[p, 8 : rows + 8, :]
                        + taps_ref[p, 1:2, lanes] * ext[p, 7 : rows + 7, :]
                        + taps_ref[p, 2:3, lanes] * ext[p, 6 : rows + 6, :]
                    ).astype(BF16)
                )
            qs, ks, vs = shorts
            qs_ref[:, lanes] = qs
            ks_ref[:, lanes] = ks
            vs_ref[:, lanes] = vs
            product = ks.astype(F32) * vs.astype(F32)
            gate = g_ref[:, lanes].astype(F32) * qs.astype(F32)
            for p in (1, 2):
                ends_ref[p - 1, :, lanes] = ext[p, rows + 6 : rows + 8, :].astype(BF16)
            blocks = pl.ds(lane // group, 128 // group)
            send_ref[blocks, 0:group, :] = product.T.astype(BF16).reshape(128 // group, group, rows)
            send_ref[blocks, group:, :] = gate.T.astype(BF16).reshape(128 // group, group, rows)
        blocks = pl.ds(chunk * size // group, size // group)
        sends.append(pltpu.make_async_copy(send_ref.at[blocks], send_hbm.at[blocks], out_sems.at[chunk]))
        sends[-1].start()
    for copy in sends:
        copy.wait()


def spectrum_kernel(own_ref, mir_ref, skip_ref, table_ref, twist_ref, out_ref, own_s, mir_s, lhs):
    channels, length = own_ref.shape
    shards = twist_ref.shape[1]
    width = length // shards
    table = table_views(table_ref, shards, width)
    first_ref, forth_ref = table["first_thrice"], table["kernel_forth"]
    scale = 1.0 / math.sqrt(length)
    first_channel = lax.axis_index("seq") * channels
    for n1 in range(shards):
        own_s[n1 * channels : (n1 + 1) * channels, :] = own_ref[:, n1 * width : (n1 + 1) * width]
        mir_s[n1 * channels : (n1 + 1) * channels, :] = mir_ref[:, n1 * width : (n1 + 1) * width].astype(F32)
    cos, sin = twist_ref[0], twist_ref[1]
    step = 4

    @pl.loop(0, channels, step=step)
    def _(base):
        for i in range(step):
            c = base + i
            own = own_s[pl.ds(c, shards, stride=channels), :]
            mir = mir_s[pl.ds(channels - 1 - c, shards, stride=channels), :].astype(BF16)
            high = own.astype(BF16)
            low = (own - high.astype(F32)).astype(BF16)
            part = dot(first_ref[...], jnp.concatenate([high, high, low], 0))
            real, imag = part[:shards], part[shards:]
            rows = pl.ds(i * shards, shards)
            lhs[rows, 0:width] = (real * cos + imag * sin).astype(BF16)
            lhs[rows, width : 2 * width] = (imag * cos - real * sin).astype(BF16)
            part = dot(table["first_twice"][...], jnp.concatenate([mir, mir], 0))
            real, imag = part[:shards], part[shards:]
            lhs[rows, 2 * width : 3 * width] = (real * cos + imag * sin).astype(BF16)
            lhs[rows, 3 * width :] = (imag * cos - real * sin).astype(BF16)
        part = dot(lhs[...], forth_ref[...]) * scale
        for i in range(step):
            c = base + i
            rows = pl.ds(c * shards, shards)
            out_ref[rows, :width] = part[i * shards : (i + 1) * shards, :width] + skip_ref[first_channel + c]
            out_ref[rows, width:] = part[i * shards : (i + 1) * shards, width:]


def signals_from(spec, shards, width, cos, sin, last_ref):
    columns = []
    for real, imag in spec:
        columns.append(
            jnp.concatenate([(real * cos - imag * sin).astype(BF16), (imag * cos + real * sin).astype(BF16)], 0)
        )
    parts = dot(last_ref[...], columns[0] if len(columns) == 1 else jnp.concatenate(columns, 1))
    return parts[:shards] + parts[shards:]


def corr_kernel(x_ref, table_ref, twist_ref, spectra_ref, mir_ref, corr_ref, xs, mir_s, lhs, spec):
    shards, both, width = x_ref.shape
    channels = both // 2
    table = table_views(table_ref, shards, width)
    first_ref, last_ref = table["first_twice"], table["last_twice"]
    scale = 1.0 / math.sqrt(shards * width)
    xs[...] = x_ref[...].reshape(shards * both, width).astype(F32)
    cos, sin = twist_ref[0], twist_ref[1]
    step = 16

    @pl.loop(0, channels, step=step)
    def _(base):
        for i in range(step):
            c = base + i
            product = xs[pl.ds(c, shards, stride=both), :].astype(BF16)
            gate = xs[pl.ds(channels + c, shards, stride=both), :].astype(BF16)
            rhs = jnp.concatenate([product, gate], 1)
            part = dot(first_ref[...], jnp.concatenate([rhs, rhs], 0))
            for j in range(2):
                real = part[:shards, j * width : (j + 1) * width]
                imag = part[shards:, j * width : (j + 1) * width]
                rows = pl.ds((2 * i + j) * shards, shards)
                lhs[rows, :width] = (real * cos + imag * sin).astype(BF16)
                lhs[rows, width:] = (imag * cos - real * sin).astype(BF16)
        both_spec = dot(lhs[...], table["forth"][...])
        spectra_ref[pl.ds(2 * base * shards, 2 * step * shards), :] = both_spec
        for i in range(step):
            pr = both_spec[2 * i * shards : (2 * i + 1) * shards, :width]
            pi = both_spec[2 * i * shards : (2 * i + 1) * shards, width:]
            gr = both_spec[(2 * i + 1) * shards : (2 * i + 2) * shards, :width]
            gi = both_spec[(2 * i + 1) * shards : (2 * i + 2) * shards, width:]
            rows = pl.ds((base + i) * shards, shards)
            corr_ref[rows, :width] = (pr * gr + pi * gi).astype(BF16)
            corr_ref[rows, width:] = (pr * gi - pi * gr).astype(BF16)
        spec[...] = dot(corr_ref[pl.ds(base * shards, step * shards), :], table["conj"][...])
        for i in range(0, step, 2):
            pairs = [
                (spec[j * shards : (j + 1) * shards, :width], spec[j * shards : (j + 1) * shards, width:])
                for j in (i, i + 1)
            ]
            part = signals_from(pairs, shards, width, cos, sin, last_ref) * scale
            for j in range(2):
                c = base + i + j
                mir_s[pl.ds(channels - 1 - c, shards, stride=channels), :] = part[:, j * width : (j + 1) * width]

    for n1 in range(shards):
        mir_ref[:, n1 * width : (n1 + 1) * width] = mir_s[n1 * channels : (n1 + 1) * channels, :].astype(BF16)


def mix_kernel(spectra_ref, spec_ref, table_ref, twist_ref, out_ref, ys, lhs, spec, first_s, extra_s):
    shards, rows_sent, width = out_ref.shape
    channels = spec_ref.shape[0] // shards
    both = 2 * channels
    table = table_views(table_ref, shards, width)
    last_ref = table["last_twice"]
    cos, sin = twist_ref[0], twist_ref[1]
    step = 16
    lane_channel = lax.broadcasted_iota(jnp.int32, (shards, width), 1) % channels
    first_s[...] = jnp.zeros_like(first_s)

    @pl.loop(0, channels, step=step)
    def _(base):
        for i in range(step):
            c = base + i
            kr = spec_ref[pl.ds(c * shards, shards), :width]
            ki = spec_ref[pl.ds(c * shards, shards), width:]
            pr = spectra_ref[pl.ds(2 * c * shards, shards), :width]
            pi = spectra_ref[pl.ds(2 * c * shards, shards), width:]
            gr = spectra_ref[pl.ds((2 * c + 1) * shards, shards), :width]
            gi = spectra_ref[pl.ds((2 * c + 1) * shards, shards), width:]
            rows = pl.ds(2 * i * shards, shards)
            lhs[rows, :width] = (kr * pr - ki * pi).astype(BF16)
            lhs[rows, width:] = (kr * pi + ki * pr).astype(BF16)
            rows = pl.ds((2 * i + 1) * shards, shards)
            lhs[rows, :width] = (kr * gr + ki * gi).astype(BF16)
            lhs[rows, width:] = (kr * gi - ki * gr).astype(BF16)
        spec[...] = dot(lhs[...], table["back"][...])
        firsts = [jnp.zeros((shards, width), F32)] * 4
        for i in range(step):
            c = base + i
            pairs = []
            for j in range(2):
                rows = slice((2 * i + j) * shards, (2 * i + j + 1) * shards)
                pairs.append((spec[rows, :width], spec[rows, width:]))
            part = signals_from(pairs, shards, width, cos, sin, last_ref)
            for j in range(2):
                ys[pl.ds(j * channels + c, shards, stride=both), :] = part[:, j * width : (j + 1) * width]
                for p in range(2):
                    column = jnp.broadcast_to(part[:, j * width + p : j * width + p + 1], (shards, width))
                    firsts[2 * j + p] = jnp.where(lane_channel == c, column, firsts[2 * j + p])
        for k in range(4):
            first_s[k, :shards, :] += firsts[k]

    out_ref[:, :both, :] = ys[...].astype(BF16).reshape(shards, both, width)
    extra_s[...] = jnp.zeros_like(extra_s)
    for k in range(4):
        extra_s[pl.ds(k, shards, stride=8), :] = first_s[k, 1 : shards + 1, :]
    out_ref[:, both:, :] = extra_s[...].astype(BF16).reshape(shards, 8, width)


def post_kernel(r_ref, g_ref, qs_ref, ks_ref, vs_ref, ends_ref, next_ref, taps_ref, mixed_hbm, q_hbm, k_hbm, v_hbm, mixed_ref, q_ref, k_ref, v_ref, ext, around, sems):
    rows, channels = g_ref.shape
    group = (r_ref.shape[1] - 8) // 2
    count = 128 // group
    shape = (count, 8, 128)
    size = channels // sems.shape[0]
    pairs = ((mixed_ref, mixed_hbm), (q_ref, q_hbm), (k_ref, k_hbm), (v_ref, v_hbm))
    copies = []
    mine = lax.broadcasted_iota(jnp.int32, shape, 2) // group == lax.broadcasted_iota(jnp.int32, shape, 0)
    for lane in range(0, channels, 128):
        lanes = pl.ds(lane, 128)
        blocks = pl.ds(lane // group, count)
        mix = r_ref[blocks, :group, :].reshape(128, rows).astype(F32).T
        back = r_ref[blocks, group : 2 * group, :].reshape(128, rows).astype(F32).T
        beyond = jnp.sum(jnp.where(mine, r_ref[blocks, 2 * group :, :].astype(F32), 0.0), 0)
        mixed_ref[:, lanes] = (qs_ref[:, lanes].astype(F32) * mix).astype(BF16)
        near = (g_ref, ks_ref, vs_ref)
        gate, key, value = [ref[:, lanes].astype(F32) for ref in near]
        gate_next = next_ref[0, :, lanes].astype(F32)
        shorts_next = []
        for p in (1, 2):
            around[0:2, :] = ends_ref[p - 1, :, lanes].astype(F32)
            around[2:4, :] = next_ref[p, :, lanes].astype(F32)
            shorts_next.append(
                (
                    taps_ref[p, 0:1, lanes] * around[2:4, :]
                    + taps_ref[p, 1:2, lanes] * around[1:3, :]
                    + taps_ref[p, 2:3, lanes] * around[0:2, :]
                )
                .astype(BF16)
                .astype(F32)
            )
        key_next, value_next = shorts_next
        parts = (gate * mix, back * value, back * key)
        beyonds = (gate_next * beyond[0:2], beyond[2:4] * value_next, beyond[2:4] * key_next)
        for p, ref in enumerate((q_ref, k_ref, v_ref)):
            ext[p, 0:rows, :] = parts[p]
            ext[p, rows : rows + 2, :] = beyonds[p]
            ref[:, lanes] = (
                taps_ref[p, 0:1, lanes] * parts[p]
                + taps_ref[p, 1:2, lanes] * ext[p, 1 : rows + 1, :]
                + taps_ref[p, 2:3, lanes] * ext[p, 2 : rows + 2, :]
            ).astype(BF16)
        if (lane + 128) % size == 0:
            chunk = lane // size
            lanes = pl.ds(chunk * size, size)
            for p, (src, dst) in enumerate(pairs):
                copies.append(pltpu.make_async_copy(src.at[:, lanes], dst.at[:, lanes], sems.at[chunk, p]))
                copies[-1].start()
    for copy in copies:
        copy.wait()


def lags_kernel(x_ref, far_ref, table_ref, twist_ref, out_ref, corr_ref, xs, own_s, lhs, spec):
    shards, both, width = x_ref.shape
    channels = both // 2
    table = table_views(table_ref, shards, width)
    first_ref, last_ref = table["first_twice"], table["last_twice"]
    scale = 1.0 / math.sqrt(shards * width)
    xs[...] = x_ref[...].reshape(shards * both, width).astype(F32)
    cos, sin = twist_ref[0], twist_ref[1]
    step = 16

    @pl.loop(0, channels, step=step)
    def _(base):
        for i in range(step):
            c = base + i
            product = xs[pl.ds(c, shards, stride=both), :].astype(BF16)
            gate = xs[pl.ds(channels + c, shards, stride=both), :].astype(BF16)
            rhs = jnp.concatenate([product, gate], 1)
            part = dot(first_ref[...], jnp.concatenate([rhs, rhs], 0))
            for j in range(2):
                real = part[:shards, j * width : (j + 1) * width]
                imag = part[shards:, j * width : (j + 1) * width]
                rows = pl.ds((2 * i + j) * shards, shards)
                lhs[rows, :width] = (real * cos + imag * sin).astype(BF16)
                lhs[rows, width:] = (imag * cos - real * sin).astype(BF16)
        both_spec = dot(lhs[...], table["forth"][...])
        for i in range(step):
            pr = both_spec[2 * i * shards : (2 * i + 1) * shards, :width]
            pi = both_spec[2 * i * shards : (2 * i + 1) * shards, width:]
            gr = both_spec[(2 * i + 1) * shards : (2 * i + 2) * shards, :width]
            gi = both_spec[(2 * i + 1) * shards : (2 * i + 2) * shards, width:]
            rows = pl.ds((base + i) * shards, shards)
            corr_ref[rows, :width] = (pr * gr + pi * gi).astype(BF16)
            corr_ref[rows, width:] = (pr * gi - pi * gr).astype(BF16)
        spec[...] = dot(corr_ref[pl.ds(base * shards, step * shards), :], table["back"][...])
        for i in range(0, step, 2):
            pairs = [
                (spec[j * shards : (j + 1) * shards, :width], spec[j * shards : (j + 1) * shards, width:])
                for j in (i, i + 1)
            ]
            part = signals_from(pairs, shards, width, cos, sin, last_ref) * scale
            for j in range(2):
                c = base + i + j
                own_s[pl.ds(c, shards, stride=channels), :] = part[:, j * width : (j + 1) * width]

    for n1 in range(shards):
        lanes = slice(n1 * width, (n1 + 1) * width)
        out_ref[:, lanes] = own_s[n1 * channels : (n1 + 1) * channels, :] + far_ref[:, lanes].astype(F32)


def per_device(query_proj, key_proj, value_proj, short_taps, skip_gain, long_filter, out_grad):
    positions, width = query_proj.shape
    channels, length = long_filter.shape
    shards = lax.axis_size("seq")
    table, twist = make_tables(shards, positions)
    shape = jax.ShapeDtypeStruct

    near = [pltpu.with_memory_space_constraint(x, pltpu.HBM) for x in (query_proj, key_proj, value_proj, out_grad)]
    ends, starts = call(
        ends_kernel,
        (shape((3, 2, width), BF16), shape((3, 2, width), BF16)),
        [pltpu.VMEM((6, 16, width), BF16), pltpu.SemaphoreType.DMA((6,))],
        bytes_accessed=200 * width,
        in_specs=[pl.BlockSpec(memory_space=pltpu.HBM)] * 4,
    )(*near)
    previous = passed_along(ends, "seq", 1)
    wide = shape((positions, width), BF16)
    hbm, vmem = pl.BlockSpec(memory_space=pltpu.HBM), pl.BlockSpec(memory_space=pltpu.VMEM)
    far = [pltpu.with_memory_space_constraint(x, pltpu.HBM) for x in (out_grad, short_taps, long_filter)]
    *staged, filter_sent = call(
        stage_kernel,
        (wide, wide, wide, wide, shape(short_taps.shape, F32), shape((channels, length), BF16)),
        [pltpu.VMEM((channels, length), F32), pltpu.SemaphoreType.DMA((6,))],
        flops=STAGE_FLOPS,
        bytes_accessed=16 * positions * width,
        in_specs=[hbm] * 6,
    )(*near[:3], *far)
    previous, filter_sent = lax.optimization_barrier((previous, filter_sent))
    filter_far = to_mirror(filter_sent)
    query_short, key_short, value_short, send, own_ends = call(
        pre_kernel,
        (wide, wide, wide, shape((shards, 2 * channels, positions), BF16), shape((2, 2, width), BF16)),
        [
            pltpu.VMEM((shards, 2 * channels, positions), BF16),
            pltpu.VMEM((3, positions + 8, 128), F32),
            pltpu.SemaphoreType.DMA((4,)),
        ],
        flops=30 * positions * width,
        bytes_accessed=18 * positions * width,
        out_specs=(vmem, vmem, vmem, hbm, vmem),
    )(*staged, previous)
    received = lax.all_to_all(send, "seq", split_axis=0, concat_axis=0, tiled=True)

    step = 16
    spectrum = call(
        spectrum_kernel,
        shape((channels * shards, 2 * positions), F32),
        [
            pltpu.VMEM((shards * channels, positions), F32),
            pltpu.VMEM((shards * channels, positions), F32),
            pltpu.VMEM((4 * shards, 4 * positions), BF16),
        ],
        flops=SPEC_FLOPS,
        bytes_accessed=14 * channels * length,
        in_specs=[pl.BlockSpec(memory_space=pltpu.VMEM)] * 2
        + [pl.BlockSpec(memory_space=pltpu.SMEM)]
        + [pl.BlockSpec(memory_space=pltpu.VMEM)] * 2,
    )(long_filter, filter_far, skip_gain, table, twist)

    received, spectrum = lax.optimization_barrier((received, spectrum))
    spectra, lagged_back = call(
        corr_kernel,
        (
            shape((2 * channels * shards, 2 * positions), F32),
            shape((channels, length), BF16),
        ),
        [
            pltpu.VMEM((channels * shards, 2 * positions), BF16),
            pltpu.VMEM((shards * 2 * channels, positions), F32),
            pltpu.VMEM((shards * channels, positions), F32),
            pltpu.VMEM((2 * step * shards, 2 * positions), BF16),
            pltpu.VMEM((step * shards, 2 * positions), F32),
        ],
        flops=CORR_FLOPS,
        bytes_accessed=24 * channels * length,
    )(received, table, twist)
    returned = call(
        mix_kernel,
        shape((shards, 2 * channels + 8, positions), BF16),
        [
            pltpu.VMEM((shards * 2 * channels, positions), F32),
            pltpu.VMEM((2 * step * shards, 2 * positions), BF16),
            pltpu.VMEM((2 * step * shards, 2 * positions), F32),
            pltpu.VMEM((4, shards + 8, positions), F32),
            pltpu.VMEM((shards * 8, positions), F32),
        ],
        flops=MIX_FLOPS,
        bytes_accessed=24 * channels * length,
    )(spectra, spectrum, table, twist)
    lagged_far = to_mirror(lagged_back)
    result = lax.all_to_all(returned, "seq", split_axis=0, concat_axis=0, tiled=True)

    starts, lagged_far = lax.optimization_barrier((starts, lagged_far))
    following = passed_along(starts, "seq", -1)
    filter_grad = call(
        lags_kernel,
        shape((channels, length), F32),
        [
            pltpu.VMEM((channels * shards, 2 * positions), BF16),
            pltpu.VMEM((shards * 2 * channels, positions), F32),
            pltpu.VMEM((shards * channels, positions), F32),
            pltpu.VMEM((2 * step * shards, 2 * positions), BF16),
            pltpu.VMEM((step * shards, 2 * positions), F32),
        ],
        flops=ADD_FLOPS,
        bytes_accessed=10 * channels * length,
    )(received, lagged_far, table, twist)
    following, filter_grad = lax.optimization_barrier((following, filter_grad))
    mixed_out, query_grad, key_grad, value_grad = call(
        post_kernel,
        (wide, wide, wide, wide),
        [
            *[pltpu.VMEM((positions, width), BF16)] * 4,
            pltpu.VMEM((3, positions + 8, 128), F32),
            pltpu.VMEM((8, 128), F32),
            pltpu.SemaphoreType.DMA((4, 4)),
        ],
        flops=30 * positions * width,
        bytes_accessed=20 * positions * width,
        out_specs=(hbm, hbm, hbm, hbm),
    )(result, out_grad, query_short, key_short, value_short, own_ends, following, short_taps)
    return (mixed_out, query_grad, key_grad, value_grad, filter_grad)


def solution(mesh):
    in_specs = (
        P("seq", "chan"),
        P("seq", "chan"),
        P("seq", "chan"),
        P(None, None, "chan"),
        P("chan"),
        P(("chan", "seq"), None),
        P("seq", "chan"),
    )
    out_specs = (
        P("seq", "chan"),
        P("seq", "chan"),
        P("seq", "chan"),
        P("seq", "chan"),
        P(("chan", "seq"), None),
    )
    return jax.shard_map(
        per_device, mesh=mesh, in_specs=in_specs, out_specs=out_specs, check_vma=False
    )
```
